128 devices in a mesh: pb: 16 (over y, x_hi, core), ka: 8 (over z, x_lo).
Axes of the slice: x: 4 (x_hi: 2, x_lo: 2; x = x_hi * 2 + x_lo), y: 4, z: 4, core: 2. Of those that a mesh axis runs over, the one named last changes fastest.
Arguments:
- bin_states: bfloat16 [8192, 1536], P(('pb', 'ka')), may hold values from -50 to 50
- contacts: int32 [8192, 16384], P('pb', 'ka'), may hold values from 0 to 2047, as said below
- w_query: bfloat16 [1536, 256], replicated, may hold values from -0.15625 to 0.15625
- w_keyval: bfloat16 [1536, 512], replicated, may hold values from -0.15625 to 0.15625
- pair_in: float32 [2, 32], replicated, may hold values from -30 to 30
- pair_shift: float32 [2, 32], replicated, may hold values from -230 to 230
- pair_out: float32 [2, 32], replicated, may hold values from -2.7 to 2.7
- w_out: bfloat16 [256, 1536], replicated, may hold values from -0.375 to 0.375
Outputs:
- mixed_out: bfloat16 [8192, 1536], P(('pb', 'ka'))
The draws below stay inside these ranges and needn't reach their ends.
Inputs may be any that keep to these rules, and one draw needn't show every extreme that they name: contacts fall off with the distance |c - 8192|; the count at offset zero reaches 2047 in every draw.
All inputs are finite; a program needn't handle non-finite values.
Results may differ from the reference program's by a relative error of at most 0.012.
The reference program's roundings to bfloat16 on the way (of `queries`, `key_values`, `weights` and `attended`) count: a program that leaves them out, or rounds other values in their place, can miss the bound.
Values may be sent and summed in bfloat16 or wider, within the bound.
A program may use at most 128 MiB of HBM per device.

```python
import math
import jax
import jax.numpy as jnp
from jax import lax

D = 1536
HEADS = 2
HEAD_DIM = 128
PAIR_HIDDEN = 32
HALF_BAND = 8192
QBLOCK = 512
SEQ = 8192


def draw_bin_states(key, part):
    values = jnp.clip(jax.random.normal(key, (SEQ, D), jnp.float32), -5.0, 5.0)
    return values.astype(jnp.bfloat16)


def draw_contacts(key, part):
    distance = jnp.abs(jnp.arange(2 * HALF_BAND, dtype=jnp.int32) - HALF_BAND)
    upper = 1 + 2047 // (1 + distance // 16)
    drawn = jax.random.randint(key, (SEQ, 2 * HALF_BAND), 0, 2 * upper[None, :])
    return jnp.minimum(drawn, upper[None, :] - 1).astype(jnp.int32)


def pair_units(key):
    base_key = jax.random.fold_in(key, 4099)
    key_list = jax.random.split(base_key, 6)
    pair_count = PAIR_HIDDEN // 2
    grid_shape = (HEADS, pair_count)
    slope_low, slope_high = (10.0, 25.0)
    centre_first, centre_reach, centre_power = (0.2, 7.0, 2.0)
    narrow_step, broad_step = (0.06, 0.2)
    slopes = jnp.exp(jax.random.uniform(key_list[0], grid_shape, jnp.float32, math.log(slope_low), math.log(slope_high)))
    flip_signs = jnp.where(jax.random.randint(key_list[1], grid_shape, 0, 2) == 0, -1.0, 1.0).astype(jnp.float32)
    centres = centre_first + centre_reach * jax.random.uniform(key_list[2], grid_shape, jnp.float32) ** centre_power
    step_widths = jax.random.uniform(key_list[3], grid_shape, jnp.float32, narrow_step, broad_step)
    height_signs = jnp.where(jax.random.randint(key_list[5], grid_shape, 0, 2) == 0, -1.0, 1.0).astype(jnp.float32)
    heights = jax.random.uniform(key_list[4], grid_shape, jnp.float32, 0.6, 1.6) * height_signs
    gain_in = flip_signs * slopes
    first_shift = -gain_in * centres
    second_shift = -gain_in * (centres + step_widths)
    scale_out = heights / (slopes * step_widths)
    unit_in = jnp.stack([gain_in, gain_in], 2).reshape(HEADS, PAIR_HIDDEN)
    unit_shift = jnp.stack([first_shift, second_shift], 2).reshape(HEADS, PAIR_HIDDEN)
    unit_out = jnp.stack([scale_out, -scale_out], 2).reshape(HEADS, PAIR_HIDDEN)
    return (unit_in.astype(jnp.float32), unit_shift.astype(jnp.float32), unit_out.astype(jnp.float32))


def draw_pair_in(key, part):
    return pair_units(key)[0]


def draw_pair_shift(key, part):
    return pair_units(key)[1]


def draw_pair_out(key, part):
    return pair_units(key)[2]


def centred(own_key, extent, width, most, kind=jnp.bfloat16):
    return jnp.clip(width * jax.random.normal(own_key, extent, jnp.float32), -most, most).astype(kind)


def setup_inputs(seed: int = 0) -> dict:
    splits = jax.random.split(jax.random.key(seed), 9)
    bin_states = draw_bin_states(jax.random.fold_in(splits[8], 71), 0)
    contacts = draw_contacts(jax.random.fold_in(splits[8], 71), 0)
    w_query = centred(splits[2], (D, HEADS * HEAD_DIM), D ** -0.5, 0.15625)
    w_keyval = centred(splits[3], (D, 2 * HEADS * HEAD_DIM), D ** -0.5, 0.15625)
    pair_in = draw_pair_in(jax.random.fold_in(splits[8], 71), 0)
    pair_shift = draw_pair_shift(jax.random.fold_in(splits[8], 71), 0)
    pair_out = draw_pair_out(jax.random.fold_in(splits[8], 71), 0)
    w_out = centred(splits[7], (HEADS * HEAD_DIM, D), (HEADS * HEAD_DIM) ** -0.5, 0.375)
    return {"bin_states": bin_states, "contacts": contacts, "w_query": w_query, "w_keyval": w_keyval, "pair_in": pair_in, "pair_shift": pair_shift, "pair_out": pair_out, "w_out": w_out}


def shear_rows(tile):
    leading, height, length = tile.shape
    padded = jnp.pad(tile, ((0, 0), (0, 0), (0, height + 1)))
    flattened = padded.reshape(leading, height * (length + height + 1))
    flattened = flattened[:, : height * (length + height)]
    return flattened.reshape(leading, height, length + height)


def pair_bias(pair_counts, pair_in, pair_shift, pair_out):
    log_counts = jnp.log(1.0 + pair_counts.astype(jnp.float32))
    per_head = []
    for head_index in range(HEADS):
        summed = jnp.zeros(log_counts.shape, jnp.float32)
        for hidden_unit in range(PAIR_HIDDEN):
            inner = pair_in[head_index, hidden_unit] * log_counts + pair_shift[head_index, hidden_unit]
            summed = summed + pair_out[head_index, hidden_unit] * jax.nn.silu(inner)
        per_head.append(summed)
    return jnp.stack(per_head, 0)


def reference(bin_states, contacts, w_query, w_keyval, pair_in, pair_shift, pair_out, w_out):
    head_cols = HEADS * HEAD_DIM
    queries = jnp.dot(bin_states, w_query, preferred_element_type=jnp.float32).astype(jnp.bfloat16)
    key_values = jnp.dot(bin_states, w_keyval, preferred_element_type=jnp.float32).astype(jnp.bfloat16)
    sub_rows = min(512, QBLOCK)
    sub_count = SEQ // sub_rows
    key_span = sub_rows + 2 * HALF_BAND
    padded = jnp.pad(key_values, ((HALF_BAND, HALF_BAND), (0, 0)))
    inv_root = 1.0 / (HEAD_DIM ** 0.5)

    def one_block(block_index):
        first_row = (block_index * sub_rows).astype(jnp.int32)
        rows_query = lax.dynamic_slice_in_dim(queries, first_row, sub_rows, 0)
        keys_here = lax.dynamic_slice_in_dim(padded, first_row, key_span, 0)
        pair_counts = lax.dynamic_slice_in_dim(contacts, first_row, sub_rows, 0)
        bias_tile = shear_rows(pair_bias(pair_counts, pair_in, pair_shift, pair_out))
        query_heads = rows_query.reshape(sub_rows, HEADS, HEAD_DIM).astype(jnp.float32)
        key_heads = keys_here[:, :head_cols].reshape(key_span, HEADS, HEAD_DIM).astype(jnp.float32)
        value_heads = keys_here[:, head_cols:].reshape(key_span, HEADS, HEAD_DIM).astype(jnp.float32)
        scores = jnp.einsum("ihd,khd->hik", query_heads, key_heads) * inv_root + bias_tile
        row_pos = jnp.arange(sub_rows, dtype=jnp.int32)[:, None]
        col_pos = jnp.arange(key_span, dtype=jnp.int32)[None, :]
        key_pos = first_row - HALF_BAND + col_pos
        allowed = (col_pos >= row_pos) & (col_pos < row_pos + 2 * HALF_BAND) & (key_pos >= 0) & (key_pos < SEQ)
        scores = jnp.where(allowed[None], scores, -1e30)
        row_top = jnp.max(scores, axis=2, keepdims=True)
        weights = jnp.exp(scores - row_top).astype(jnp.bfloat16)
        totals = jnp.sum(weights.astype(jnp.float32), axis=2)
        numerators = jnp.einsum("hik,khd->ihd", weights.astype(jnp.float32), value_heads)
        attended = numerators / jnp.transpose(totals)[:, :, None]
        return attended.reshape(sub_rows, head_cols).astype(jnp.bfloat16)

    attended = lax.map(one_block, jnp.arange(sub_count, dtype=jnp.int32))
    attended = attended.reshape(SEQ, head_cols)
    return jnp.dot(attended, w_out, preferred_element_type=jnp.float32).astype(jnp.bfloat16)
```

```python
import functools
import jax
import jax.numpy as jnp
from jax import lax
from jax.experimental import pallas as pl
from jax.experimental.pallas import tpu as pltpu
from jax.sharding import PartitionSpec as P

HEADS = 2
HEAD_DIM = 128
PAIR_HIDDEN = 32
HALF_BAND = 8192
SEGS = 16
ROOT = HEAD_DIM**0.5
LOG2E = 1.4426950408889634
NEG = -1e30
MESH = pl.DeviceIdType.MESH
F32 = jnp.float32
BF16 = jnp.bfloat16


def gather_kernel(
    pbn, kan, x_ref, wq_ref, wkv_ref, q_out, win_out,
    qs, kvs, q_send, q_recv, kv_send, kv_recv, f_send, f_recv,
):
    p = lax.axis_index("pb")
    k = lax.axis_index("ka")
    rows = x_ref.shape[0]
    block = rows * kan
    partner = p + 1 - 2 * (p % 2)
    first = p + 4 * k - 16

    def dest(kd, m):
        pd = p - 4 * kd + 16 - 2 * m
        return pd, (pd >= 0) & (pd < pbn)

    def has(m):
        b = first + 2 * m
        return (b >= 0) & (b < pbn)

    barrier = pltpu.get_barrier_semaphore()
    for i in range(1, kan):
        pl.semaphore_signal(
            barrier, inc=1, device_id=(p, lax.rem(k + i, kan)), device_id_type=MESH
        )
    pl.semaphore_signal(barrier, inc=1, device_id=(partner, k), device_id_type=MESH)
    for m in range(3):
        b = first + 2 * m
        for i in range(kan):
            own = (b == p) & (i == 0)

            @pl.when(has(m) & jnp.logical_not(own))
            def _(b=b, i=i):
                pl.semaphore_signal(
                    barrier, inc=1, device_id=(b, lax.rem(k + i, kan)), device_id_type=MESH
                )

    qs[...] = jnp.dot(x_ref[...], wq_ref[...], preferred_element_type=F32).astype(BF16)
    kvs[...] = jnp.dot(x_ref[...], wkv_ref[...], preferred_element_type=F32).astype(BF16)

    expected = kan
    for i in range(kan):
        kd = lax.rem(k + i, kan)
        for m in range(3):
            pd, ok = dest(kd, m)
            own = (pd == p) & (i == 0)
            expected = expected + jnp.where(ok & jnp.logical_not(own), 1, 0)
    pl.semaphore_wait(barrier, expected)

    def q_copy(i):
        kd = lax.rem(k + i, kan)
        return pltpu.make_async_remote_copy(
            src_ref=qs, dst_ref=q_out.at[pl.ds(k * rows, rows)],
            send_sem=q_send.at[i], recv_sem=q_recv,
            device_id=(p, kd), device_id_type=MESH,
        )

    def kv_rows(m):
        return win_out.at[pl.ds(2 * m * block + k * rows, rows)]

    def kv_copy(i, m, pd, kd):
        return pltpu.make_async_remote_copy(
            src_ref=kvs, dst_ref=kv_rows(m),
            send_sem=kv_send.at[i, m], recv_sem=kv_recv.at[m],
            device_id=(pd, kd), device_id_type=MESH,
        )

    for i in range(kan):
        kd = lax.rem(k + i, kan)
        for m in range(3):
            pd, ok = dest(kd, m)
            own = (pd == p) & (i == 0)

            @pl.when(ok & jnp.logical_not(own))
            def _(i=i, m=m, pd=pd, kd=kd):
                kv_copy(i, m, pd, kd).start()

            if i == 0:

                @pl.when(ok & own)
                def _(m=m):
                    pltpu.make_async_copy(kvs, kv_rows(m), kv_recv.at[m]).start()

        if i:
            q_copy(i).start()
    own_q = pltpu.make_async_copy(qs, q_out.at[pl.ds(k * rows, rows)], q_recv)
    own_q.start()

    odd = p % 2

    def fwd(slot):
        m = slot + 1 - odd
        return pltpu.make_async_remote_copy(
            src_ref=win_out.at[pl.ds(2 * m * block, block)],
            dst_ref=win_out.at[pl.ds((2 * slot + 1) * block, block)],
            send_sem=f_send.at[slot], recv_sem=f_recv.at[slot],
            device_id=(partner, k), device_id_type=MESH,
        )

    def in_block(m):
        part = win_out.at[pl.ds(2 * m * block, block)]
        return pltpu.make_async_remote_copy(
            src_ref=part, dst_ref=part, send_sem=kv_send.at[0, m], recv_sem=kv_recv.at[m],
            device_id=(partner, k), device_id_type=MESH,
        )

    for m in range(3):

        @pl.when(has(m))
        def _(m=m):
            in_block(m).wait_recv()

        for slot in range(2):
            b = first + 2 * m

            @pl.when(has(m) & (slot + 1 - odd == m))
            def _(slot=slot):
                fwd(slot).start()

    for slot in range(2):
        b_in = first + 2 * slot + 1

        @pl.when((b_in >= 0) & (b_in < pbn))
        def _(slot=slot):
            fwd(slot).wait_recv()

        b_out = first + 2 * (slot + 1 - odd)

        @pl.when((b_out >= 0) & (b_out < pbn))
        def _(slot=slot):
            fwd(slot).wait_send()

    for i in range(kan):
        kd = lax.rem(k + i, kan)
        for m in range(3):
            pd, ok = dest(kd, m)
            own = (pd == p) & (i == 0)

            @pl.when(ok & jnp.logical_not(own))
            def _(i=i, m=m, pd=pd, kd=kd):
                kv_copy(i, m, pd, kd).wait_send()

        if i:
            q_copy(i).wait_send()
    whole = pltpu.make_async_remote_copy(
        src_ref=q_out, dst_ref=q_out, send_sem=q_send.at[0], recv_sem=q_recv,
        device_id=(partner, k), device_id_type=MESH,
    )
    whole.wait_recv()


def attend_kernel(
    tiles, blocks, start_ref, pin_ref, psh_ref, pout_ref, con_ref, q_ref, win_ref, msg_ref,
    tab, bias, smax, sbuf, acc, seen, fix,
):
    rb = pl.program_id(0)
    first = start_ref[0]
    lanes = lax.broadcasted_iota(jnp.int32, (128, 128), 1)
    subl = lax.broadcasted_iota(jnp.int32, (128, 128), 0)
    here = lanes >= subl
    pad = 4

    @pl.when(rb == 0)
    def _():
        ids = (
            lax.broadcasted_iota(jnp.int32, (SEGS, 128), 0) * 128
            + lax.broadcasted_iota(jnp.int32, (SEGS, 128), 1)
        )
        logc = jnp.log(1.0 + ids.astype(F32))
        for h in range(HEADS):
            summed = jnp.zeros((SEGS, 128), F32)
            for u in range(PAIR_HIDDEN):
                inner = pin_ref[h, u] * logc + psh_ref[h, u]
                summed = summed + pout_ref[h, u] * (inner / (1.0 + jnp.exp(-inner)))
            summed = summed * ROOT
            for s in range(SEGS):
                tab[h, s] = jnp.broadcast_to(summed[s : s + 1], (8, 128))
            bias[h, :, 0 : pad * 128] = jnp.full((128, pad * 128), NEG, F32)
            bias[h, :, (pad + tiles) * 128 : (2 * pad + tiles) * 128] = jnp.full(
                (128, pad * 128), NEG, F32
            )

    lo = jnp.maximum(0, -first)
    hi = jnp.minimum(tiles // 4 + 1, blocks - first)
    active = hi > lo

    smax[...] = jnp.full(smax.shape, NEG, F32)
    acc[...] = jnp.zeros(acc.shape, F32)

    def pick(table, low):
        dims = lax.GatherDimensionNumbers(
            offset_dims=(), collapsed_slice_dims=(1,), start_index_map=(1,),
            operand_batching_dims=(0,), start_indices_batching_dims=(0,),
        )
        return lax.gather(
            table, low[:, :, None], dims, slice_sizes=(1, 1),
            mode=lax.GatherScatterMode.PROMISE_IN_BOUNDS,
        )

    def roll(x):
        return pltpu.roll(x, 0, 1, stride=1, stride_axis=0)

    @pl.when(active)
    def _():
        tables = [tab[h, 0] for h in range(HEADS)]

        def look(it, every):
            for u in range(4):
                at = pl.multiple_of((it * 4 + u) * 128, 128)
                c = con_ref[:, pl.ds(at, 128)]
                some = functools.reduce(
                    jnp.bitwise_or, [c[8 * g : 8 * g + 8] for g in range(16)]
                )
                seen[it * 4 + u] = some
                every = every | some
                low = roll(c & 127)
                for g in range(16):
                    for h in range(HEADS):
                        bias[h, 8 * g : 8 * g + 8, pl.ds(at + pad * 128, 128)] = pick(
                            tables[h], low[8 * g : 8 * g + 8]
                        )
            return every

        every = lax.fori_loop(0, tiles // 4, look, jnp.zeros((8, 128), jnp.int32))

        @pl.when(jnp.max(every.astype(F32)) > 127.5)
        def _():
            def tile(j, _):
                most = jnp.max(seen[j].astype(F32))

                @pl.when(most > 127.5)
                def _():
                    at = pl.multiple_of(j * 128, 128)
                    fix[...] = jnp.zeros(fix.shape, F32)
                    rounds = (most.astype(jnp.int32) >> 9) + 1

                    def some_rows(r, _):
                        for g in range(16):
                            c = con_ref[8 * g : 8 * g + 8, pl.ds(at, 128)]
                            low = c & 127
                            row = c >> 7
                            for h in range(HEADS):
                                got = fix[h, 8 * g : 8 * g + 8]
                                for u in range(4):
                                    got = jnp.where(
                                        row == 4 * r + u, pick(tab[h, 4 * r + u], low), got
                                    )
                                fix[h, 8 * g : 8 * g + 8] = got
                        return 0

                    lax.fori_loop(0, rounds, some_rows, 0)
                    for h in range(HEADS):
                        bias[h, :, pl.ds(at + pad * 128, 128)] = roll(fix[h])

                return 0

            lax.fori_loop(0, tiles, tile, 0)

        q = q_ref[...]

        def score(j, _):
            for h in range(HEADS):
                keys = win_ref[
                    pl.ds(pl.multiple_of(j * 512, 512), 512), 128 * h : 128 * h + 128
                ]
                s = jnp.dot(q[:, 128 * h : 128 * h + 128], keys.T, preferred_element_type=F32)
                top = smax[h]
                for i in range(4):
                    at = pl.multiple_of((pad + 4 * j + i - rb) * 128, 128)
                    b = jnp.where(here, bias[h, :, pl.ds(at, 128)], bias[h, :, pl.ds(at - 128, 128)])
                    part = s[:, 128 * i : 128 * i + 128] + b
                    sbuf[h, :, pl.ds(pl.multiple_of((4 * j + i) * 128, 128), 128)] = part
                    top = jnp.maximum(top, part)
                smax[h] = top
            return 0

        lax.fori_loop(lo, hi, score, 0)
        for h in range(HEADS):
            smax[h] = jnp.broadcast_to(jnp.max(smax[h], axis=1, keepdims=True), (128, 128))
        ones = jnp.ones((512, 128), BF16)

        def weigh(j, _):
            vals = win_ref[pl.ds(pl.multiple_of(j * 512, 512), 512), 256:512]
            for h in range(HEADS):
                w = []
                for i in range(4):
                    s = sbuf[h, :, pl.ds(pl.multiple_of((4 * j + i) * 128, 128), 128)]
                    w.append(jnp.exp2((s - smax[h]) * (LOG2E / ROOT)).astype(BF16))
                v = jnp.concatenate([vals[:, 128 * h : 128 * h + 128], ones], 1)
                acc[h] += jnp.dot(jnp.concatenate(w, 1), v, preferred_element_type=F32)
            return 0

        lax.fori_loop(lo, hi, weigh, 0)

    stats = jnp.zeros((128, 128), F32)
    for h in range(HEADS):
        msg_ref[:, 128 * h : 128 * h + 128] = acc[h, :, 0:128].astype(BF16)
        for n, full in enumerate((smax[h] * (1.0 / ROOT), acc[h, :, 128:256])):
            for part in range(3):
                piece = full.astype(BF16).astype(F32)
                stats = jnp.where(lanes == h * 6 + n * 3 + part, piece, stats)
                full = full - piece
    msg_ref[:, 256:384] = stats.astype(BF16)


def reduce_kernel(pbn, kan, msg_ref, wo_ref, out_ref, slots, send, recv):
    p = lax.axis_index("pb")
    k = lax.axis_index("ka")
    rows = out_ref.shape[0]

    def active(kd):
        b0 = p + 4 * kd - 16
        return (b0 >= -4) & (b0 < pbn)

    barrier = pltpu.get_barrier_semaphore()
    for i in range(1, kan):
        kd = lax.rem(k + i, kan)

        @pl.when(active(kd))
        def _(kd=kd):
            pl.semaphore_signal(barrier, inc=1, device_id=(p, kd), device_id_type=MESH)

    def copy(i):
        kd = lax.rem(k + i, kan)
        return pltpu.make_async_remote_copy(
            src_ref=msg_ref.at[pl.ds(kd * rows, rows)], dst_ref=slots.at[i],
            send_sem=send.at[i], recv_sem=recv.at[i],
            device_id=(p, kd), device_id_type=MESH,
        )

    @pl.when(active(k))
    def _():
        pl.semaphore_wait(barrier, kan - 1)
        for i in range(1, kan):
            copy(i).start()

    own = msg_ref[pl.ds(k * rows, rows), :].astype(F32)
    slots[0] = own.astype(BF16)
    for i in range(1, kan):
        src = lax.rem(k + kan - i, kan)

        @pl.when(active(src))
        def _(i=i):
            copy(i).wait_recv()

        @pl.when(jnp.logical_not(active(src)))
        def _(i=i):
            slots[i] = jnp.zeros(slots.shape[1:], BF16)

    res = []
    for h in range(HEADS):
        tops, tots, nums = [], [], []
        for i in range(kan):
            st = slots[i, :, 256:384].astype(F32)
            live = active(lax.rem(k + kan - i, kan))
            a = 6 * h
            top = st[:, a : a + 1] + st[:, a + 1 : a + 2] + st[:, a + 2 : a + 3]
            tops.append(jnp.where(live, top, NEG))
            tots.append(st[:, a + 3 : a + 4] + st[:, a + 4 : a + 5] + st[:, a + 5 : a + 6])
            nums.append(slots[i, :, 128 * h : 128 * h + 128].astype(F32))
        top = functools.reduce(jnp.maximum, tops)
        num = jnp.zeros((rows, HEAD_DIM), F32)
        tot = jnp.zeros((rows, 1), F32)
        for i in range(kan):
            w = jnp.exp(tops[i] - top)
            num = num + w * nums[i]
            tot = tot + w * tots[i]
        res.append((num / tot).astype(BF16))
    att = jnp.concatenate(res, 1)
    out_ref[...] = jnp.dot(att, wo_ref[...], preferred_element_type=F32).astype(BF16)

    @pl.when(active(k))
    def _():
        for i in range(1, kan):
            copy(i).wait_send()


def shards(pbn, kan, bin_states, contacts, w_query, w_keyval, pair_in, pair_shift, pair_out, w_out):
    vmem = pl.BlockSpec(memory_space=pltpu.VMEM)
    smem = pl.BlockSpec(memory_space=pltpu.SMEM)
    hbm = pl.BlockSpec(memory_space=pl.ANY)
    rows, width = bin_states.shape
    block, offsets = contacts.shape
    hc = HEADS * HEAD_DIM
    window = block + offsets
    q_blk, win = pl.pallas_call(
        functools.partial(gather_kernel, pbn, kan),
        out_shape=(
            jax.ShapeDtypeStruct((block, hc), BF16),
            jax.ShapeDtypeStruct((window, 2 * hc), BF16),
        ),
        in_specs=[vmem, vmem, vmem],
        out_specs=(hbm, hbm),
        scratch_shapes=[
            pltpu.VMEM((rows, hc), BF16),
            pltpu.VMEM((rows, 2 * hc), BF16),
            pltpu.SemaphoreType.DMA((kan,)),
            pltpu.SemaphoreType.DMA,
            pltpu.SemaphoreType.DMA((kan, 3)),
            pltpu.SemaphoreType.DMA((3,)),
            pltpu.SemaphoreType.DMA((2,)),
            pltpu.SemaphoreType.DMA((2,)),
        ],
        compiler_params=pltpu.CompilerParams(collective_id=0, has_side_effects=True),
        name="gather_windows",
    )(bin_states, w_query, w_keyval)

    p = lax.axis_index("pb")
    k = lax.axis_index("ka")
    start = ((p * block + k * offsets - HALF_BAND) // block).astype(jnp.int32).reshape(1)
    tiles = offsets // 128
    rb_count = block // 128
    msg = pl.pallas_call(
        functools.partial(attend_kernel, tiles, pbn),
        grid=(rb_count,),
        out_shape=jax.ShapeDtypeStruct((block, hc + 128), BF16),
        in_specs=[
            smem, smem, smem, smem,
            pl.BlockSpec((128, offsets), lambda r: (r, 0)),
            pl.BlockSpec((128, hc), lambda r: (r, 0)),
            pl.BlockSpec((window, 2 * hc), lambda r: (0, 0), pipeline_mode=pl.Buffered(1)),
        ],
        out_specs=pl.BlockSpec((128, hc + 128), lambda r: (r, 0)),
        scratch_shapes=[
            pltpu.VMEM((HEADS, SEGS, 8, 128), F32),
            pltpu.VMEM((HEADS, 128, (tiles + 8) * 128), F32),
            pltpu.VMEM((HEADS, 128, 128), F32),
            pltpu.VMEM((HEADS, 128, (tiles + 4) * 128), F32),
            pltpu.VMEM((HEADS, 128, 256), F32),
            pltpu.VMEM((tiles, 8, 128), jnp.int32),
            pltpu.VMEM((HEADS, 128, 128), F32),
        ],
        name="attend",
    )(start, pair_in, pair_shift, pair_out, contacts, q_blk, win)

    return pl.pallas_call(
        functools.partial(reduce_kernel, pbn, kan),
        out_shape=jax.ShapeDtypeStruct((rows, width), BF16),
        in_specs=[vmem, vmem],
        out_specs=vmem,
        scratch_shapes=[
            pltpu.VMEM((kan, rows, hc + 128), BF16),
            pltpu.SemaphoreType.DMA((kan,)),
            pltpu.SemaphoreType.DMA((kan,)),
        ],
        compiler_params=pltpu.CompilerParams(collective_id=1, has_side_effects=True),
        name="reduce_rows",
    )(msg, w_out)


def solution(mesh):
    placed = (P(("pb", "ka"), None), P("pb", "ka"), P(), P(), P(), P(), P(), P())
    return jax.shard_map(
        functools.partial(shards, mesh.shape["pb"], mesh.shape["ka"]),
        mesh=mesh, in_specs=placed, out_specs=P(("pb", "ka"), None), check_vma=False,
    )
```

```python
import functools
import jax
import jax.numpy as jnp
from jax import lax
from jax.experimental import pallas as pl
from jax.experimental.pallas import tpu as pltpu
from jax.sharding import PartitionSpec as P

HEADS = 2
HEAD_DIM = 128
PAIR_HIDDEN = 32
HALF_BAND = 8192
SEGS = 16
ROOT = HEAD_DIM**0.5
LOG2E = 1.4426950408889634
NEG = -1e30
MESH = pl.DeviceIdType.MESH
F32 = jnp.float32
BF16 = jnp.bfloat16


def pick(table, low):
    dims = lax.GatherDimensionNumbers(
        offset_dims=(), collapsed_slice_dims=(1,), start_index_map=(1,),
        operand_batching_dims=(0,), start_indices_batching_dims=(0,),
    )
    return lax.gather(
        table, low[:, :, None], dims, slice_sizes=(1, 1),
        mode=lax.GatherScatterMode.PROMISE_IN_BOUNDS,
    )


def shear(x):
    return pltpu.roll(x, 0, 1, stride=1, stride_axis=0)


def build_table(pin_ref, psh_ref, pout_ref, tab):
    ids = (
        lax.broadcasted_iota(jnp.int32, (SEGS, 128), 0) * 128
        + lax.broadcasted_iota(jnp.int32, (SEGS, 128), 1)
    )
    logc = jnp.log(1.0 + ids.astype(F32))
    for h in range(HEADS):
        summed = jnp.zeros((SEGS, 128), F32)
        for u in range(PAIR_HIDDEN):
            inner = pin_ref[h, u] * logc + psh_ref[h, u]
            summed = summed + pout_ref[h, u] * (inner / (1.0 + jnp.exp(-inner)))
        summed = summed * ROOT
        for s in range(SEGS):
            tab[h, s] = jnp.broadcast_to(summed[s : s + 1], (8, 128))


def message(rows, tops, sums, msg_ref):
    lanes = lax.broadcasted_iota(jnp.int32, (128, 128), 1)
    stats = jnp.zeros((128, 128), F32)
    for h in range(HEADS):
        msg_ref[rows, 128 * h : 128 * h + 128] = sums[h][:, 0:128].astype(BF16)
        for n, full in enumerate((tops[h] * (1.0 / ROOT), sums[h][:, 128:256])):
            for part in range(3):
                piece = full.astype(BF16).astype(F32)
                stats = jnp.where(lanes == h * 6 + n * 3 + part, piece, stats)
                full = full - piece
    msg_ref[rows, 256:384] = stats.astype(BF16)


def main_kernel(
    pbn, kan, pin_ref, psh_ref, pout_ref, x_hbm, wq_hbm, wkv_hbm, con_hbm,
    msg_ref, odd_ref, q_out, win_out,
    x, wq, wkv, con, qs, kvs, qall, win, tab, bias, sbuf, wbuf, tops, alpha, acc,
    in_sem, con_sem, q_send, q_recv, kv_send, kv_recv, f_send, f_recv, out_sem,
):
    p = lax.axis_index("pb")
    k = lax.axis_index("ka")
    rows = x.shape[0]
    block = rows * kan
    tiles = con.shape[1] // 128
    partner = p + 1 - 2 * (p % 2)
    odd = p % 2
    first = p + 4 * k - 16
    pad = 4
    active = (first >= -4) & (first < pbn)

    loads = [
        pltpu.make_async_copy(x_hbm, x, in_sem.at[0]),
        pltpu.make_async_copy(wkv_hbm, wkv, in_sem.at[1]),
        pltpu.make_async_copy(wq_hbm, wq, in_sem.at[2]),
    ]
    for c in loads:
        c.start()

    def con_load(r):
        at = pl.ds(r * 128, 128)
        return pltpu.make_async_copy(con_hbm.at[at], con.at[at], con_sem.at[r])

    for r in range(4):
        con_load(r).start()

    def dest(kd, m):
        pd = p - 4 * kd + 16 - 2 * m
        return pd, (pd >= 0) & (pd < pbn)

    def has(m):
        b = first + 2 * m
        return (b >= 0) & (b < pbn)

    barrier = pltpu.get_barrier_semaphore()
    for i in range(1, kan):
        pl.semaphore_signal(
            barrier, inc=1, device_id=(p, lax.rem(k + i, kan)), device_id_type=MESH
        )
    pl.semaphore_signal(barrier, inc=1, device_id=(partner, k), device_id_type=MESH)
    for m in range(3):
        b = first + 2 * m
        for i in range(kan):
            own = (b == p) & (i == 0)

            @pl.when(has(m) & jnp.logical_not(own))
            def _(b=b, i=i):
                pl.semaphore_signal(
                    barrier, inc=1, device_id=(b, lax.rem(k + i, kan)), device_id_type=MESH
                )

    expected = kan
    for i in range(kan):
        kd = lax.rem(k + i, kan)
        for m in range(3):
            pd, ok = dest(kd, m)
            own = (pd == p) & (i == 0)
            expected = expected + jnp.where(ok & jnp.logical_not(own), 1, 0)

    loads[0].wait()
    loads[1].wait()
    kvs[...] = jnp.dot(x[...], wkv[...], preferred_element_type=F32).astype(BF16)
    pl.semaphore_wait(barrier, expected)

    def q_copy(i):
        kd = lax.rem(k + i, kan)
        return pltpu.make_async_remote_copy(
            src_ref=qs, dst_ref=qall.at[pl.ds(k * rows, rows)],
            send_sem=q_send.at[i], recv_sem=q_recv,
            device_id=(p, kd), device_id_type=MESH,
        )

    def kv_rows(m):
        return win.at[pl.ds(2 * m * block + k * rows, rows)]

    def kv_copy(i, m, pd, kd):
        return pltpu.make_async_remote_copy(
            src_ref=kvs, dst_ref=kv_rows(m),
            send_sem=kv_send.at[i, m], recv_sem=kv_recv.at[m],
            device_id=(pd, kd), device_id_type=MESH,
        )

    def send_kv(m):
        for i in range(kan):
            kd = lax.rem(k + i, kan)
            pd, ok = dest(kd, m)
            own = (pd == p) & (i == 0)

            @pl.when(ok & jnp.logical_not(own))
            def _(i=i, m=m, pd=pd, kd=kd):
                kv_copy(i, m, pd, kd).start()

            if i == 0:

                @pl.when(ok & own)
                def _(m=m):
                    pltpu.make_async_copy(kvs, kv_rows(m), kv_recv.at[m]).start()

    send_kv(0)
    loads[2].wait()
    qs[...] = jnp.dot(x[...], wq[...], preferred_element_type=F32).astype(BF16)
    for i in range(1, kan):
        q_copy(i).start()
    pltpu.make_async_copy(qs, qall.at[pl.ds(k * rows, rows)], q_recv).start()
    send_kv(1)
    send_kv(2)

    def fwd(slot):
        m = slot + 1 - odd
        return pltpu.make_async_remote_copy(
            src_ref=win.at[pl.ds(2 * m * block, block)],
            dst_ref=win.at[pl.ds((2 * slot + 1) * block, block)],
            send_sem=f_send.at[slot], recv_sem=f_recv.at[slot],
            device_id=(partner, k), device_id_type=MESH,
        )

    def in_block(m):
        part = win.at[pl.ds(2 * m * block, block)]
        return pltpu.make_async_remote_copy(
            src_ref=part, dst_ref=part, send_sem=kv_send.at[0, m], recv_sem=kv_recv.at[m],
            device_id=(partner, k), device_id_type=MESH,
        )

    def keep(j):
        at = pl.ds(j * block, block)
        return pltpu.make_async_copy(win.at[at], win_out.at[at], out_sem.at[j])

    lanes = lax.broadcasted_iota(jnp.int32, (128, 128), 1)
    subl = lax.broadcasted_iota(jnp.int32, (128, 128), 0)
    here = lanes >= subl

    @pl.when(active)
    def _():
        build_table(pin_ref, psh_ref, pout_ref, tab)
        tables = [tab[h, 0] for h in range(HEADS)]
        near = jnp.where(k == 4, 0, jnp.where(k == 3, tiles - 1, -1))
        second = jnp.where(k == 4, 1, jnp.where(k == 3, tiles - 2, -1))

        for r in range(4):
            con_load(r).wait()

        def look_rows(r, every):
            at_r = pl.multiple_of(r * 128, 128)
            band = pl.ds(at_r, 128)
            edge = jnp.full((128, pad * 128), NEG, F32)
            for h in range(HEADS):
                bias[h, band, 0 : pad * 128] = edge
                bias[h, band, (pad + tiles) * 128 : (2 * pad + tiles) * 128] = edge

            def look(it, every):
                for u in range(4):
                    j = it * 4 + u
                    at = pl.multiple_of(j * 128, 128)
                    c = con[band, pl.ds(at, 128)]
                    some = functools.reduce(
                        jnp.bitwise_or, [c[8 * g : 8 * g + 8] for g in range(16)]
                    )
                    beyond = jnp.where(j == near, 0, jnp.where(j == second, -512, -128))
                    every = every | (some & beyond)
                    low = shear(c & 127)
                    for g in range(16):
                        for h in range(HEADS):
                            bias[
                                h, pl.ds(at_r + 8 * g, 8), pl.ds(at + pad * 128, 128)
                            ] = pick(tables[h], low[8 * g : 8 * g + 8])
                return every

            every = lax.fori_loop(0, tiles // 4, look, every)

            def further(j, rounds):
                at = pl.multiple_of(j * 128, 128)
                c = shear(con[band, pl.ds(at, 128)])

                def some_rows(t, _):
                    for g in range(16):
                        low = c[8 * g : 8 * g + 8] & 127
                        row = c[8 * g : 8 * g + 8] >> 7
                        for h in range(HEADS):
                            part = (h, pl.ds(at_r + 8 * g, 8), pl.ds(at + pad * 128, 128))
                            got = bias[part]
                            for u in range(4):
                                got = jnp.where(
                                    row == 4 * t + u, pick(tab[h, 4 * t + u], low), got
                                )
                            bias[part] = got
                    return 0

                lax.fori_loop(0, rounds, some_rows, 0)

            @pl.when(near >= 0)
            def _():
                further(near, SEGS // 4)
                further(second, 1)

            return every

        odd_ref[...] = lax.fori_loop(0, 4, look_rows, jnp.zeros((8, 128), jnp.int32))
        tops[...] = jnp.full(tops.shape, NEG, F32)
        acc[...] = jnp.zeros(acc.shape, F32)

    whole = pltpu.make_async_remote_copy(
        src_ref=qall, dst_ref=qall, send_sem=q_send.at[0], recv_sem=q_recv,
        device_id=(partner, k), device_id_type=MESH,
    )
    whole.wait_recv()
    q_keep = pltpu.make_async_copy(qall, q_out, out_sem.at[5])
    q_keep.start()
    ones = jnp.ones((block, 128), BF16)

    def attend(j):
        at_k = pl.multiple_of(j * block, block)
        for h in range(HEADS):
            keys = win[pl.ds(at_k, block), 128 * h : 128 * h + 128]
            s = jnp.dot(
                qall[:, 128 * h : 128 * h + 128], keys.T, preferred_element_type=F32
            )
            for r in range(4):
                band = slice(128 * r, 128 * r + 128)
                most = None
                for i in range(4):
                    at = pl.multiple_of((pad + 4 * j + i - r) * 128, 128)
                    b = jnp.where(
                        here, bias[h, band, pl.ds(at, 128)], bias[h, band, pl.ds(at - 128, 128)]
                    )
                    part = s[band, 128 * i : 128 * i + 128] + b
                    sbuf[h, band, 128 * i : 128 * i + 128] = part
                    most = part if most is None else jnp.maximum(most, part)
                top = tops[h, band, :]
                new = jnp.maximum(top, jnp.max(most, axis=1, keepdims=True))
                alpha[h, band, :] = jnp.exp2((top - new) * (LOG2E / ROOT))
                tops[h, band, :] = new
                for i in range(4):
                    wbuf[h, band, 128 * i : 128 * i + 128] = jnp.exp2(
                        (sbuf[h, band, 128 * i : 128 * i + 128] - new) * (LOG2E / ROOT)
                    ).astype(BF16)
            vals = win[pl.ds(at_k, block), 256 + 128 * h : 384 + 128 * h]
            new = jnp.dot(
                wbuf[h], jnp.concatenate([vals, ones], 1), preferred_element_type=F32
            )
            a = alpha[h]
            acc[h] = acc[h] * jnp.concatenate([a, a], 1) + new

    def step(it, _):
        j = lax.rem(2 * it, 5)
        b = first + j

        @pl.when((b >= 0) & (b < pbn))
        def _():
            @pl.when(it < 3)
            def _():
                in_block(it).wait_recv()
                slot = it - 1 + odd

                @pl.when((slot >= 0) & (slot < 2))
                def _():
                    fwd(slot).start()

            @pl.when(it >= 3)
            def _():
                fwd(it - 3).wait_recv()

            keep(j).start()
            attend(j)

        return 0

    lax.fori_loop(0, 5, step, 0)

    @pl.when(active)
    def _():
        def finish(r, _):
            band = pl.ds(pl.multiple_of(r * 128, 128), 128)
            message(
                band, [tops[h, band, :] for h in range(HEADS)],
                [acc[h, band, :] for h in range(HEADS)], msg_ref,
            )
            return 0

        lax.fori_loop(0, 4, finish, 0)

    @pl.when(jnp.logical_not(active))
    def _():
        odd_ref[...] = jnp.zeros((8, 128), jnp.int32)
        msg_ref[...] = jnp.zeros(msg_ref.shape, BF16)
        for r in range(4):
            con_load(r).wait()

    def drain(j, _):
        b = first + j

        @pl.when((b >= 0) & (b < pbn))
        def _():
            keep(j).wait()

        return 0

    lax.fori_loop(0, 5, drain, 0)
    q_keep.wait()
    for slot in range(2):
        b_out = first + 2 * (slot + 1 - odd)

        @pl.when((b_out >= 0) & (b_out < pbn))
        def _(slot=slot):
            fwd(slot).wait_send()

    for i in range(kan):
        kd = lax.rem(k + i, kan)
        for m in range(3):
            pd, ok = dest(kd, m)
            own = (pd == p) & (i == 0)

            @pl.when(ok & jnp.logical_not(own))
            def _(i=i, m=m, pd=pd, kd=kd):
                kv_copy(i, m, pd, kd).wait_send()

        if i:
            q_copy(i).wait_send()


def redo_kernel(
    tiles, blocks, start_ref, odd_ref, pin_ref, psh_ref, pout_ref, con_hbm, q_hbm, win_hbm, msg_in,
    msg_out, tab, con, q, win, bias, smax, sbuf, acc, msg, sem,
):
    first = start_ref[0]
    pad = 4

    @pl.when(jnp.max(odd_ref[...].astype(F32)) > 0.5)
    def _():
        lanes = lax.broadcasted_iota(jnp.int32, (128, 128), 1)
        subl = lax.broadcasted_iota(jnp.int32, (128, 128), 0)
        here = lanes >= subl
        build_table(pin_ref, psh_ref, pout_ref, tab)
        lo = jnp.maximum(0, -first)
        hi = jnp.minimum(tiles // 4 + 1, blocks - first)
        edge = jnp.full((128, pad * 128), NEG, F32)
        for h in range(HEADS):
            bias[h, :, 0 : pad * 128] = edge
            bias[h, :, (pad + tiles) * 128 : (2 * pad + tiles) * 128] = edge

        def fetch(src, dst):
            c = pltpu.make_async_copy(src, dst, sem)
            c.start()
            c.wait()

        def load_win(j, _):
            at = pl.ds(pl.multiple_of(j * 512, 512), 512)
            fetch(win_hbm.at[at], win.at[at])
            return 0

        lax.fori_loop(lo, hi, load_win, 0)
        ones = jnp.ones((512, 128), BF16)

        def rows(rb, _):
            band = pl.ds(pl.multiple_of(rb * 128, 128), 128)
            fetch(con_hbm.at[band], con)
            fetch(q_hbm.at[band], q)
            smax[...] = jnp.full(smax.shape, NEG, F32)
            acc[...] = jnp.zeros(acc.shape, F32)

            def look(j, _):
                at = pl.multiple_of(j * 128, 128)
                c = shear(con[:, pl.ds(at, 128)])

                def row(s, _):
                    for g in range(16):
                        part = c[8 * g : 8 * g + 8]
                        for h in range(HEADS):
                            spot = (h, slice(8 * g, 8 * g + 8), pl.ds(at + pad * 128, 128))
                            bias[spot] = jnp.where(
                                (part >> 7) == s, pick(tab[h, s], part & 127), bias[spot]
                            )
                    return 0

                lax.fori_loop(0, SEGS, row, 0)
                return 0

            lax.fori_loop(0, tiles, look, 0)

            def score(j, _):
                for h in range(HEADS):
                    keys = win[
                        pl.ds(pl.multiple_of(j * 512, 512), 512), 128 * h : 128 * h + 128
                    ]
                    s = jnp.dot(
                        q[:, 128 * h : 128 * h + 128], keys.T, preferred_element_type=F32
                    )
                    top = smax[h]
                    for i in range(4):
                        at = pl.multiple_of((pad + 4 * j + i - rb) * 128, 128)
                        b = jnp.where(
                            here, bias[h, :, pl.ds(at, 128)], bias[h, :, pl.ds(at - 128, 128)]
                        )
                        part = s[:, 128 * i : 128 * i + 128] + b
                        sbuf[h, :, pl.ds(pl.multiple_of((4 * j + i) * 128, 128), 128)] = part
                        top = jnp.maximum(top, part)
                    smax[h] = top
                return 0

            lax.fori_loop(lo, hi, score, 0)
            for h in range(HEADS):
                smax[h] = jnp.broadcast_to(jnp.max(smax[h], axis=1, keepdims=True), (128, 128))

            def weigh(j, _):
                for h in range(HEADS):
                    vals = win[
                        pl.ds(pl.multiple_of(j * 512, 512), 512), 256 + 128 * h : 384 + 128 * h
                    ]
                    w = []
                    for i in range(4):
                        s = sbuf[h, :, pl.ds(pl.multiple_of((4 * j + i) * 128, 128), 128)]
                        w.append(jnp.exp2((s - smax[h]) * (LOG2E / ROOT)).astype(BF16))
                    acc[h] += jnp.dot(
                        jnp.concatenate(w, 1), jnp.concatenate([vals, ones], 1),
                        preferred_element_type=F32,
                    )
                return 0

            lax.fori_loop(lo, hi, weigh, 0)
            message(
                slice(0, 128), [smax[h] for h in range(HEADS)],
                [acc[h] for h in range(HEADS)], msg,
            )
            fetch(msg, msg_out.at[band])
            return 0

        lax.fori_loop(0, 4, rows, 0)


def reduce_kernel(pbn, kan, msg_ref, wo_ref, out_ref, slots, send, recv):
    p = lax.axis_index("pb")
    k = lax.axis_index("ka")
    rows = out_ref.shape[0]

    def active(kd):
        b0 = p + 4 * kd - 16
        return (b0 >= -4) & (b0 < pbn)

    barrier = pltpu.get_barrier_semaphore()
    for i in range(1, kan):
        kd = lax.rem(k + i, kan)

        @pl.when(active(kd))
        def _(kd=kd):
            pl.semaphore_signal(barrier, inc=1, device_id=(p, kd), device_id_type=MESH)

    def copy(i):
        kd = lax.rem(k + i, kan)
        return pltpu.make_async_remote_copy(
            src_ref=msg_ref.at[pl.ds(kd * rows, rows)], dst_ref=slots.at[i],
            send_sem=send.at[i], recv_sem=recv.at[i],
            device_id=(p, kd), device_id_type=MESH,
        )

    @pl.when(active(k))
    def _():
        pl.semaphore_wait(barrier, kan - 1)
        for i in range(1, kan):
            copy(i).start()

    own = msg_ref[pl.ds(k * rows, rows), :].astype(F32)
    slots[0] = own.astype(BF16)
    for i in range(1, kan):
        src = lax.rem(k + kan - i, kan)

        @pl.when(active(src))
        def _(i=i):
            copy(i).wait_recv()

        @pl.when(jnp.logical_not(active(src)))
        def _(i=i):
            slots[i] = jnp.zeros(slots.shape[1:], BF16)

    res = []
    for h in range(HEADS):
        tops, tots, nums = [], [], []
        for i in range(kan):
            st = slots[i, :, 256:384].astype(F32)
            live = active(lax.rem(k + kan - i, kan))
            a = 6 * h
            top = st[:, a : a + 1] + st[:, a + 1 : a + 2] + st[:, a + 2 : a + 3]
            tops.append(jnp.where(live, top, NEG))
            tots.append(st[:, a + 3 : a + 4] + st[:, a + 4 : a + 5] + st[:, a + 5 : a + 6])
            nums.append(slots[i, :, 128 * h : 128 * h + 128].astype(F32))
        top = functools.reduce(jnp.maximum, tops)
        num = jnp.zeros((rows, HEAD_DIM), F32)
        tot = jnp.zeros((rows, 1), F32)
        for i in range(kan):
            w = jnp.exp(tops[i] - top)
            num = num + w * nums[i]
            tot = tot + w * tots[i]
        res.append((num / tot).astype(BF16))
    att = jnp.concatenate(res, 1)
    out_ref[...] = jnp.dot(att, wo_ref[...], preferred_element_type=F32).astype(BF16)

    @pl.when(active(k))
    def _():
        for i in range(1, kan):
            copy(i).wait_send()


def shards(pbn, kan, bin_states, contacts, w_query, w_keyval, pair_in, pair_shift, pair_out, w_out):
    vmem = pl.BlockSpec(memory_space=pltpu.VMEM)
    smem = pl.BlockSpec(memory_space=pltpu.SMEM)
    hbm = pl.BlockSpec(memory_space=pl.ANY)
    rows, width = bin_states.shape
    block, offsets = contacts.shape
    hc = HEADS * HEAD_DIM
    window = block + offsets
    tiles = offsets // 128
    msg, odd, q_blk, win = pl.pallas_call(
        functools.partial(main_kernel, pbn, kan),
        out_shape=(
            jax.ShapeDtypeStruct((block, hc + 128), BF16),
            jax.ShapeDtypeStruct((8, 128), jnp.int32),
            jax.ShapeDtypeStruct((block, hc), BF16),
            jax.ShapeDtypeStruct((window, 2 * hc), BF16),
        ),
        in_specs=[smem, smem, smem, hbm, hbm, hbm, hbm],
        out_specs=(vmem, vmem, hbm, hbm),
        scratch_shapes=[
            pltpu.VMEM((rows, width), BF16),
            pltpu.VMEM((width, hc), BF16),
            pltpu.VMEM((width, 2 * hc), BF16),
            pltpu.VMEM((block, offsets), jnp.int32),
            pltpu.VMEM((rows, hc), BF16),
            pltpu.VMEM((rows, 2 * hc), BF16),
            pltpu.VMEM((block, hc), BF16),
            pltpu.VMEM((window, 2 * hc), BF16),
            pltpu.VMEM((HEADS, SEGS, 8, 128), F32),
            pltpu.VMEM((HEADS, block, (tiles + 8) * 128), F32),
            pltpu.VMEM((HEADS, block, block), F32),
            pltpu.VMEM((HEADS, block, block), BF16),
            pltpu.VMEM((HEADS, block, 128), F32),
            pltpu.VMEM((HEADS, block, 128), F32),
            pltpu.VMEM((HEADS, block, 256), F32),
            pltpu.SemaphoreType.DMA((3,)),
            pltpu.SemaphoreType.DMA((4,)),
            pltpu.SemaphoreType.DMA((kan,)),
            pltpu.SemaphoreType.DMA,
            pltpu.SemaphoreType.DMA((kan, 3)),
            pltpu.SemaphoreType.DMA((3,)),
            pltpu.SemaphoreType.DMA((2,)),
            pltpu.SemaphoreType.DMA((2,)),
            pltpu.SemaphoreType.DMA((6,)),
        ],
        compiler_params=pltpu.CompilerParams(collective_id=0, has_side_effects=True),
        name="gather_attend",
    )(pair_in, pair_shift, pair_out, bin_states, w_query, w_keyval, contacts)

    p = lax.axis_index("pb")
    k = lax.axis_index("ka")
    start = ((p * block + k * offsets - HALF_BAND) // block).astype(jnp.int32).reshape(1)
    msg = pl.pallas_call(
        functools.partial(redo_kernel, tiles, pbn),
        out_shape=jax.ShapeDtypeStruct((block, hc + 128), BF16),
        in_specs=[smem, vmem, smem, smem, smem, hbm, hbm, hbm, hbm],
        out_specs=hbm,
        scratch_shapes=[
            pltpu.VMEM((HEADS, SEGS, 8, 128), F32),
            pltpu.VMEM((128, offsets), jnp.int32),
            pltpu.VMEM((128, hc), BF16),
            pltpu.VMEM((window, 2 * hc), BF16),
            pltpu.VMEM((HEADS, 128, (tiles + 8) * 128), F32),
            pltpu.VMEM((HEADS, 128, 128), F32),
            pltpu.VMEM((HEADS, 128, (tiles + 4) * 128), F32),
            pltpu.VMEM((HEADS, 128, 256), F32),
            pltpu.VMEM((128, hc + 128), BF16),
            pltpu.SemaphoreType.DMA,
        ],
        input_output_aliases={8: 0},
        name="redo",
    )(start, odd, pair_in, pair_shift, pair_out, contacts, q_blk, win, msg)

    return pl.pallas_call(
        functools.partial(reduce_kernel, pbn, kan),
        out_shape=jax.ShapeDtypeStruct((rows, width), BF16),
        in_specs=[vmem, vmem],
        out_specs=vmem,
        scratch_shapes=[
            pltpu.VMEM((kan, rows, hc + 128), BF16),
            pltpu.SemaphoreType.DMA((kan,)),
            pltpu.SemaphoreType.DMA((kan,)),
        ],
        compiler_params=pltpu.CompilerParams(collective_id=1, has_side_effects=True),
        name="reduce_rows",
    )(msg, w_out)


def solution(mesh):
    placed = (P(("pb", "ka"), None), P("pb", "ka"), P(), P(), P(), P(), P(), P())
    return jax.shard_map(
        functools.partial(shards, mesh.shape["pb"], mesh.shape["ka"]),
        mesh=mesh, in_specs=placed, out_specs=P(("pb", "ka"), None), check_vma=False,
    )
```

```python
import functools
import jax
import jax.numpy as jnp
from jax import lax
from jax.experimental import pallas as pl
from jax.experimental.pallas import tpu as pltpu
from jax.sharding import PartitionSpec as P

HEADS = 2
HEAD_DIM = 128
PAIR_HIDDEN = 32
HALF_BAND = 8192
SEGS = 16
ROOT = HEAD_DIM**0.5
LOG2E = 1.4426950408889634
NEG = -1e30
MESH = pl.DeviceIdType.MESH
F32 = jnp.float32
BF16 = jnp.bfloat16


def pick(table, low):
    dims = lax.GatherDimensionNumbers(
        offset_dims=(), collapsed_slice_dims=(1,), start_index_map=(1,),
        operand_batching_dims=(0,), start_indices_batching_dims=(0,),
    )
    return lax.gather(
        table, low[:, :, None], dims, slice_sizes=(1, 1),
        mode=lax.GatherScatterMode.PROMISE_IN_BOUNDS,
    )


def shear(x):
    return pltpu.roll(x, 0, 1, stride=1, stride_axis=0)


def build_table(pin_ref, psh_ref, pout_ref, tab):
    ids = (
        lax.broadcasted_iota(jnp.int32, (SEGS, 128), 0) * 128
        + lax.broadcasted_iota(jnp.int32, (SEGS, 128), 1)
    )
    logc = jnp.log(1.0 + ids.astype(F32))
    for h in range(HEADS):
        summed = jnp.zeros((SEGS, 128), F32)
        for u in range(PAIR_HIDDEN):
            inner = pin_ref[h, u] * logc + psh_ref[h, u]
            summed = summed + pout_ref[h, u] * (inner / (1.0 + jnp.exp(-inner)))
        summed = summed * ROOT
        for s in range(SEGS):
            tab[h, s] = jnp.broadcast_to(summed[s : s + 1], (8, 128))


def message(rows, tops, sums, num_ref, stat_ref):
    lanes = lax.broadcasted_iota(jnp.int32, (128, 128), 1)
    stats = jnp.zeros((128, 128), F32)
    for h in range(HEADS):
        num_ref[rows, 128 * h : 128 * h + 128] = sums[h][:, 0:128].astype(BF16)
        for n, full in enumerate((tops[h] * (1.0 / ROOT), sums[h][:, 128:256])):
            for part in range(3):
                piece = full.astype(BF16).astype(F32)
                stats = jnp.where(lanes == h * 6 + n * 3 + part, piece, stats)
                full = full - piece
    stat_ref[...] = stats.T[0:16, :].astype(BF16)


def main_kernel(
    pbn, kan, pin_ref, psh_ref, pout_ref, x_hbm, wq_hbm, wkv_hbm, con_hbm,
    num_ref, stat_ref, odd_ref, q_out, win_out,
    x, wq, wkv, con, qs, kvs, qall, win, tab, bias, sbuf, wbuf, tops, alpha, acc,
    in_sem, con_sem, q_send, q_recv, kv_send, kv_recv, f_send, f_recv, out_sem,
):
    p = lax.axis_index("pb")
    k = lax.axis_index("ka")
    rows = x.shape[0]
    block = rows * kan
    tiles = con.shape[1] // 128
    partner = p + 1 - 2 * (p % 2)
    odd = p % 2
    first = p + 4 * k - 16
    pad = 4
    active = (first >= -4) & (first < pbn)

    loads = [
        pltpu.make_async_copy(x_hbm, x, in_sem.at[0]),
        pltpu.make_async_copy(wkv_hbm, wkv, in_sem.at[1]),
        pltpu.make_async_copy(wq_hbm, wq, in_sem.at[2]),
    ]
    for c in loads:
        c.start()

    def con_load(r):
        at = pl.ds(r * 128, 128)
        return pltpu.make_async_copy(con_hbm.at[at], con.at[at], con_sem.at[r])

    def dest(kd, m):
        pd = p - 4 * kd + 16 - 2 * m
        return pd, (pd >= 0) & (pd < pbn)

    def has(m):
        b = first + 2 * m
        return (b >= 0) & (b < pbn)

    barrier = pltpu.get_barrier_semaphore()
    for i in range(1, kan):
        pl.semaphore_signal(
            barrier, inc=1, device_id=(p, lax.rem(k + i, kan)), device_id_type=MESH
        )
    pl.semaphore_signal(barrier, inc=1, device_id=(partner, k), device_id_type=MESH)
    for m in range(3):
        b = first + 2 * m
        for i in range(kan):
            own = (b == p) & (i == 0)

            @pl.when(has(m) & jnp.logical_not(own))
            def _(b=b, i=i):
                pl.semaphore_signal(
                    barrier, inc=1, device_id=(b, lax.rem(k + i, kan)), device_id_type=MESH
                )

    expected = kan
    for i in range(kan):
        kd = lax.rem(k + i, kan)
        for m in range(3):
            pd, ok = dest(kd, m)
            own = (pd == p) & (i == 0)
            expected = expected + jnp.where(ok & jnp.logical_not(own), 1, 0)

    @pl.when(active)
    def _():
        build_table(pin_ref, psh_ref, pout_ref, tab)
        edge = jnp.full((block, (pad + 1) * 128), NEG, F32)
        for h in range(HEADS):
            bias[h, :, 0 : (pad + 1) * 128] = edge
            bias[h, :, (pad + tiles) * 128 : (2 * pad + tiles) * 128] = edge[:, 128:]
        tops[...] = jnp.full(tops.shape, NEG, F32)
        acc[...] = jnp.zeros(acc.shape, F32)

    loads[0].wait()
    loads[1].wait()
    for r in range(4):
        con_load(r).start()
    kvs[...] = jnp.dot(x[...], wkv[...], preferred_element_type=F32).astype(BF16)
    pl.semaphore_wait(barrier, expected)

    def q_copy(i):
        kd = lax.rem(k + i, kan)
        return pltpu.make_async_remote_copy(
            src_ref=qs, dst_ref=qall.at[pl.ds(k * rows, rows)],
            send_sem=q_send.at[i], recv_sem=q_recv,
            device_id=(p, kd), device_id_type=MESH,
        )

    def kv_rows(m):
        return win.at[pl.ds(2 * m * block + k * rows, rows)]

    def kv_copy(i, m, pd, kd):
        return pltpu.make_async_remote_copy(
            src_ref=kvs, dst_ref=kv_rows(m),
            send_sem=kv_send.at[i, m], recv_sem=kv_recv.at[m],
            device_id=(pd, kd), device_id_type=MESH,
        )

    def send_kv(m):
        for i in range(kan):
            kd = lax.rem(k + i, kan)
            pd, ok = dest(kd, m)
            own = (pd == p) & (i == 0)

            @pl.when(ok & jnp.logical_not(own))
            def _(i=i, m=m, pd=pd, kd=kd):
                kv_copy(i, m, pd, kd).start()

            if i == 0:

                @pl.when(ok & own)
                def _(m=m):
                    pltpu.make_async_copy(kvs, kv_rows(m), kv_recv.at[m]).start()

    send_kv(0)
    loads[2].wait()
    qs[...] = jnp.dot(x[...], wq[...], preferred_element_type=F32).astype(BF16)
    def wanted(i):
        b0 = p + 4 * lax.rem(k + i, kan) - 16
        return (b0 >= -4) & (b0 < pbn)

    for i in range(1, kan):

        @pl.when(wanted(i))
        def _(i=i):
            q_copy(i).start()

    @pl.when(active)
    def _():
        pltpu.make_async_copy(qs, qall.at[pl.ds(k * rows, rows)], q_recv).start()

    send_kv(1)
    send_kv(2)

    def fwd(slot):
        m = slot + 1 - odd
        return pltpu.make_async_remote_copy(
            src_ref=win.at[pl.ds(2 * m * block, block)],
            dst_ref=win.at[pl.ds((2 * slot + 1) * block, block)],
            send_sem=f_send.at[slot], recv_sem=f_recv.at[slot],
            device_id=(partner, k), device_id_type=MESH,
        )

    def in_block(m):
        part = win.at[pl.ds(2 * m * block, block)]
        return pltpu.make_async_remote_copy(
            src_ref=part, dst_ref=part, send_sem=kv_send.at[0, m], recv_sem=kv_recv.at[m],
            device_id=(partner, k), device_id_type=MESH,
        )

    def keep(j):
        at = pl.ds(j * block, block)
        return pltpu.make_async_copy(win.at[at], win_out.at[at], out_sem.at[j])

    lanes = lax.broadcasted_iota(jnp.int32, (128, 128), 1)
    subl = lax.broadcasted_iota(jnp.int32, (128, 128), 0)
    here = lanes >= subl

    @pl.when(active)
    def _():
        tables = [tab[h, 0] for h in range(HEADS)]
        near = jnp.where(k == 4, 0, jnp.where(k == 3, tiles - 1, -1))
        second = jnp.where(k == 4, 1, jnp.where(k == 3, tiles - 2, -1))

        for r in range(4):
            con_load(r).wait()

        def put(h, row, at, g, val):
            where = pl.ds(row, 8)
            mask = here[8 * g : 8 * g + 8]
            at = at + pad * 128
            pltpu.store(bias.at[h, where, pl.ds(at, 128)], val, mask=mask)
            pltpu.store(bias.at[h, where, pl.ds(at + 128, 128)], val, mask=jnp.logical_not(mask))

        def look_rows(r, every):
            at_r = pl.multiple_of(r * 128, 128)
            band = pl.ds(at_r, 128)
            def look(it, every):
                for u in range(4):
                    j = it * 4 + u
                    at = pl.multiple_of(j * 128, 128)
                    c = con[band, pl.ds(at, 128)]
                    some = functools.reduce(
                        jnp.bitwise_or, [c[8 * g : 8 * g + 8] for g in range(16)]
                    )
                    beyond = jnp.where(j == near, 0, jnp.where(j == second, -512, -128))
                    every = every | (some & beyond)
                    low = shear(c & 127)
                    for g in range(16):
                        for h in range(HEADS):
                            put(h, at_r + 8 * g, at, g, pick(tables[h], low[8 * g : 8 * g + 8]))
                return every

            every = lax.fori_loop(0, tiles // 4, look, every)

            def further(j, count):
                at = pl.multiple_of(j * 128, 128)
                c = shear(con[band, pl.ds(at, 128)])
                for g in range(16):
                    low = c[8 * g : 8 * g + 8] & 127
                    row = c[8 * g : 8 * g + 8] >> 7
                    got = [pick(tables[h], low) for h in range(HEADS)]
                    for u in range(1, count):
                        hit = row == u
                        for h in range(HEADS):
                            got[h] = jnp.where(hit, pick(tab[h, u], low), got[h])
                    for h in range(HEADS):
                        put(h, at_r + 8 * g, at, g, got[h])

            @pl.when(near >= 0)
            def _():
                further(near, SEGS)
                further(second, 4)

            return every

        odd_ref[...] = lax.fori_loop(0, 4, look_rows, jnp.zeros((8, 128), jnp.int32))

    whole = pltpu.make_async_remote_copy(
        src_ref=qall, dst_ref=qall, send_sem=q_send.at[0], recv_sem=q_recv,
        device_id=(partner, k), device_id_type=MESH,
    )
    q_keep = pltpu.make_async_copy(qall, q_out, out_sem.at[5])

    @pl.when(active)
    def _():
        whole.wait_recv()
        q_keep.start()

    ones = jnp.ones((block, 128), BF16)

    def attend(j, outside):
        at_k = pl.multiple_of(j * block, block)
        for h in range(HEADS):
            keys = win[pl.ds(at_k, block), 128 * h : 128 * h + 128]
            s = jnp.dot(
                qall[:, 128 * h : 128 * h + 128], keys.T, preferred_element_type=F32
            )
            for r in range(4):
                band = slice(128 * r, 128 * r + 128)
                used = [i for i in range(4) if not outside(i, r)]
                most = None
                for i in used:
                    at = pl.multiple_of((pad + 4 * j + i - r) * 128, 128)
                    part = s[band, 128 * i : 128 * i + 128] + bias[h, band, pl.ds(at, 128)]
                    sbuf[h, band, 128 * i : 128 * i + 128] = part
                    most = part if most is None else jnp.maximum(most, part)
                top = tops[h, band, :]
                new = jnp.maximum(top, jnp.max(most, axis=1, keepdims=True))
                alpha[h, band, :] = jnp.exp2((top - new) * (LOG2E / ROOT))
                tops[h, band, :] = new
                for i in range(4):
                    spot = (h, band, slice(128 * i, 128 * i + 128))
                    if i in used:
                        wbuf[spot] = jnp.exp2((sbuf[spot] - new) * (LOG2E / ROOT)).astype(BF16)
                    else:
                        wbuf[spot] = jnp.zeros((128, 128), BF16)
            vals = win[pl.ds(at_k, block), 256 + 128 * h : 384 + 128 * h]
            new = jnp.dot(
                wbuf[h], jnp.concatenate([vals, ones], 1), preferred_element_type=F32
            )
            a = alpha[h]
            acc[h] = acc[h] * jnp.concatenate([a, a], 1) + new

    def step(it, _):
        j = lax.rem(2 * it, 5)
        b = first + j

        @pl.when((b >= 0) & (b < pbn))
        def _():
            @pl.when(it < 3)
            def _():
                in_block(it).wait_recv()
                slot = it - 1 + odd

                @pl.when((slot >= 0) & (slot < 2))
                def _():
                    fwd(slot).start()

            @pl.when(it >= 3)
            def _():
                fwd(it - 3).wait_recv()

            keep(j).start()

            @pl.when(j == 0)
            def _():
                attend(j, lambda i, r: i < r)

            @pl.when(j == 4)
            def _():
                attend(j, lambda i, r: i > r)

            @pl.when((j > 0) & (j < 4))
            def _():
                attend(j, lambda i, r: False)

        return 0

    lax.fori_loop(0, 5, step, 0)

    @pl.when(active)
    def _():
        def finish(r, _):
            band = pl.ds(pl.multiple_of(r * 128, 128), 128)
            message(
                band, [tops[h, band, :] for h in range(HEADS)],
                [acc[h, band, :] for h in range(HEADS)], num_ref, stat_ref.at[r],
            )
            return 0

        lax.fori_loop(0, 4, finish, 0)

    @pl.when(jnp.logical_not(active))
    def _():
        odd_ref[...] = jnp.zeros((8, 128), jnp.int32)
        num_ref[...] = jnp.zeros(num_ref.shape, BF16)
        stat_ref[...] = jnp.zeros(stat_ref.shape, BF16)
        for r in range(4):
            con_load(r).wait()

    def drain(j, _):
        b = first + j

        @pl.when((b >= 0) & (b < pbn))
        def _():
            keep(j).wait()

        return 0

    lax.fori_loop(0, 5, drain, 0)

    @pl.when(active)
    def _():
        q_keep.wait()

    for slot in range(2):
        b_out = first + 2 * (slot + 1 - odd)

        @pl.when((b_out >= 0) & (b_out < pbn))
        def _(slot=slot):
            fwd(slot).wait_send()

    for i in range(kan):
        kd = lax.rem(k + i, kan)
        for m in range(3):
            pd, ok = dest(kd, m)
            own = (pd == p) & (i == 0)

            @pl.when(ok & jnp.logical_not(own))
            def _(i=i, m=m, pd=pd, kd=kd):
                kv_copy(i, m, pd, kd).wait_send()

        if i:

            @pl.when(wanted(i))
            def _(i=i):
                q_copy(i).wait_send()


def redo_kernel(
    tiles, blocks, start_ref, odd_ref, pin_ref, psh_ref, pout_ref, con_hbm, q_hbm, win_hbm, num_in,
    stat_in, num_out, stat_out, tab, con, q, win, bias, smax, sbuf, acc, num, stat, sem,
):
    first = start_ref[0]
    pad = 4

    @pl.when(jnp.max(odd_ref[...].astype(F32)) > 0.5)
    def _():
        lanes = lax.broadcasted_iota(jnp.int32, (128, 128), 1)
        subl = lax.broadcasted_iota(jnp.int32, (128, 128), 0)
        here = lanes >= subl
        build_table(pin_ref, psh_ref, pout_ref, tab)
        lo = jnp.maximum(0, -first)
        hi = jnp.minimum(tiles // 4 + 1, blocks - first)
        edge = jnp.full((128, pad * 128), NEG, F32)
        for h in range(HEADS):
            bias[h, :, 0 : pad * 128] = edge
            bias[h, :, (pad + tiles) * 128 : (2 * pad + tiles) * 128] = edge

        def fetch(src, dst):
            c = pltpu.make_async_copy(src, dst, sem)
            c.start()
            c.wait()

        def load_win(j, _):
            at = pl.ds(pl.multiple_of(j * 512, 512), 512)
            fetch(win_hbm.at[at], win.at[at])
            return 0

        lax.fori_loop(lo, hi, load_win, 0)
        ones = jnp.ones((512, 128), BF16)

        def rows(rb, _):
            band = pl.ds(pl.multiple_of(rb * 128, 128), 128)
            fetch(con_hbm.at[band], con)
            fetch(q_hbm.at[band], q)
            smax[...] = jnp.full(smax.shape, NEG, F32)
            acc[...] = jnp.zeros(acc.shape, F32)

            def look(j, _):
                at = pl.multiple_of(j * 128, 128)
                c = shear(con[:, pl.ds(at, 128)])

                def row(s, _):
                    for g in range(16):
                        part = c[8 * g : 8 * g + 8]
                        for h in range(HEADS):
                            spot = (h, slice(8 * g, 8 * g + 8), pl.ds(at + pad * 128, 128))
                            bias[spot] = jnp.where(
                                (part >> 7) == s, pick(tab[h, s], part & 127), bias[spot]
                            )
                    return 0

                lax.fori_loop(0, SEGS, row, 0)
                return 0

            lax.fori_loop(0, tiles, look, 0)

            def score(j, _):
                for h in range(HEADS):
                    keys = win[
                        pl.ds(pl.multiple_of(j * 512, 512), 512), 128 * h : 128 * h + 128
                    ]
                    s = jnp.dot(
                        q[:, 128 * h : 128 * h + 128], keys.T, preferred_element_type=F32
                    )
                    top = smax[h]
                    for i in range(4):
                        at = pl.multiple_of((pad + 4 * j + i - rb) * 128, 128)
                        b = jnp.where(
                            here, bias[h, :, pl.ds(at, 128)], bias[h, :, pl.ds(at - 128, 128)]
                        )
                        part = s[:, 128 * i : 128 * i + 128] + b
                        sbuf[h, :, pl.ds(pl.multiple_of((4 * j + i) * 128, 128), 128)] = part
                        top = jnp.maximum(top, part)
                    smax[h] = top
                return 0

            lax.fori_loop(lo, hi, score, 0)
            for h in range(HEADS):
                smax[h] = jnp.broadcast_to(jnp.max(smax[h], axis=1, keepdims=True), (128, 128))

            def weigh(j, _):
                for h in range(HEADS):
                    vals = win[
                        pl.ds(pl.multiple_of(j * 512, 512), 512), 256 + 128 * h : 384 + 128 * h
                    ]
                    w = []
                    for i in range(4):
                        s = sbuf[h, :, pl.ds(pl.multiple_of((4 * j + i) * 128, 128), 128)]
                        w.append(jnp.exp2((s - smax[h]) * (LOG2E / ROOT)).astype(BF16))
                    acc[h] += jnp.dot(
                        jnp.concatenate(w, 1), jnp.concatenate([vals, ones], 1),
                        preferred_element_type=F32,
                    )
                return 0

            lax.fori_loop(lo, hi, weigh, 0)
            message(
                slice(0, 128), [smax[h] for h in range(HEADS)],
                [acc[h] for h in range(HEADS)], num, stat,
            )
            fetch(num, num_out.at[band])
            fetch(stat, stat_out.at[rb])
            return 0

        lax.fori_loop(0, 4, rows, 0)


def reduce_kernel(pbn, kan, num_ref, stat_ref, out_ref, nums, stats, send, recv, st_send, st_recv):
    p = lax.axis_index("pb")
    k = lax.axis_index("ka")
    rows = out_ref.shape[0]

    def active(kd):
        b0 = p + 4 * kd - 16
        return (b0 >= -4) & (b0 < pbn)

    barrier = pltpu.get_barrier_semaphore()
    for i in range(1, kan):
        kd = lax.rem(k + i, kan)

        @pl.when(active(kd))
        def _(kd=kd):
            pl.semaphore_signal(barrier, inc=1, device_id=(p, kd), device_id_type=MESH)

    def copies(i):
        kd = lax.rem(k + i, kan)
        to = {"device_id": (p, kd), "device_id_type": MESH}
        return (
            pltpu.make_async_remote_copy(
                src_ref=stat_ref.at[kd // 2], dst_ref=stats.at[i],
                send_sem=st_send.at[i], recv_sem=st_recv.at[i], **to,
            ),
            pltpu.make_async_remote_copy(
                src_ref=num_ref.at[pl.ds(kd * rows, rows)], dst_ref=nums.at[i],
                send_sem=send.at[i], recv_sem=recv.at[i], **to,
            ),
        )

    @pl.when(active(k))
    def _():
        pl.semaphore_wait(barrier, kan - 1)
        for i in range(1, kan):
            for c in copies(i):
                c.start()

    nums[0] = num_ref[pl.ds(pl.multiple_of(k * rows, rows), rows), :]
    stats[0] = stat_ref[k // 2]
    for i in range(1, kan):
        src = lax.rem(k + kan - i, kan)

        @pl.when(active(src))
        def _(i=i):
            copies(i)[0].wait_recv()

        @pl.when(jnp.logical_not(active(src)))
        def _(i=i):
            nums[i] = jnp.zeros(nums.shape[1:], BF16)
            stats[i] = jnp.zeros(stats.shape[1:], BF16)

    shares = []
    for h in range(HEADS):
        tops, tots = [], []
        for i in range(kan):
            st = stats[i].astype(F32)
            live = active(lax.rem(k + kan - i, kan))
            a = 6 * h
            top = st[a : a + 1] + st[a + 1 : a + 2] + st[a + 2 : a + 3]
            tops.append(jnp.where(live, top, NEG))
            tots.append(st[a + 3 : a + 4] + st[a + 4 : a + 5] + st[a + 5 : a + 6])
        top = functools.reduce(jnp.maximum, tops)
        w = [jnp.exp(t - top) for t in tops]
        tot = functools.reduce(jnp.add, [a * b for a, b in zip(w, tots)])
        shares += [a / tot for a in w]
    cols = jnp.concatenate(shares + [jnp.zeros((128 - len(shares), 128), F32)], 0).T
    cols = jnp.where(lax.rem(k, 2) == 0, cols[0:rows], cols[rows : 2 * rows])

    for i in range(1, kan):

        @pl.when(active(lax.rem(k + kan - i, kan)))
        def _(i=i):
            copies(i)[1].wait_recv()

    for h in range(HEADS):
        num = jnp.zeros((rows, HEAD_DIM), F32)
        for i in range(kan):
            at = kan * h + i
            num = num + cols[:, at : at + 1] * nums[i, :, 128 * h : 128 * h + 128].astype(F32)
        out_ref[:, 128 * h : 128 * h + 128] = num.astype(BF16)

    @pl.when(active(k))
    def _():
        for i in range(1, kan):
            for c in copies(i):
                c.wait_send()


def shards(pbn, kan, bin_states, contacts, w_query, w_keyval, pair_in, pair_shift, pair_out, w_out):
    vmem = pl.BlockSpec(memory_space=pltpu.VMEM)
    smem = pl.BlockSpec(memory_space=pltpu.SMEM)
    hbm = pl.BlockSpec(memory_space=pl.ANY)
    rows, width = bin_states.shape
    block, offsets = contacts.shape
    hc = HEADS * HEAD_DIM
    window = block + offsets
    tiles = offsets // 128
    num, stat, odd, q_blk, win = pl.pallas_call(
        functools.partial(main_kernel, pbn, kan),
        out_shape=(
            jax.ShapeDtypeStruct((block, hc), BF16),
            jax.ShapeDtypeStruct((block // 128, 16, 128), BF16),
            jax.ShapeDtypeStruct((8, 128), jnp.int32),
            jax.ShapeDtypeStruct((block, hc), BF16),
            jax.ShapeDtypeStruct((window, 2 * hc), BF16),
        ),
        in_specs=[smem, smem, smem, hbm, hbm, hbm, hbm],
        out_specs=(vmem, vmem, vmem, hbm, hbm),
        scratch_shapes=[
            pltpu.VMEM((rows, width), BF16),
            pltpu.VMEM((width, hc), BF16),
            pltpu.VMEM((width, 2 * hc), BF16),
            pltpu.VMEM((block, offsets), jnp.int32),
            pltpu.VMEM((rows, hc), BF16),
            pltpu.VMEM((rows, 2 * hc), BF16),
            pltpu.VMEM((block, hc), BF16),
            pltpu.VMEM((window, 2 * hc), BF16),
            pltpu.VMEM((HEADS, SEGS, 8, 128), F32),
            pltpu.VMEM((HEADS, block, (tiles + 8) * 128), F32),
            pltpu.VMEM((HEADS, block, block), F32),
            pltpu.VMEM((HEADS, block, block), BF16),
            pltpu.VMEM((HEADS, block, 128), F32),
            pltpu.VMEM((HEADS, block, 128), F32),
            pltpu.VMEM((HEADS, block, 256), F32),
            pltpu.SemaphoreType.DMA((3,)),
            pltpu.SemaphoreType.DMA((4,)),
            pltpu.SemaphoreType.DMA((kan,)),
            pltpu.SemaphoreType.DMA,
            pltpu.SemaphoreType.DMA((kan, 3)),
            pltpu.SemaphoreType.DMA((3,)),
            pltpu.SemaphoreType.DMA((2,)),
            pltpu.SemaphoreType.DMA((2,)),
            pltpu.SemaphoreType.DMA((6,)),
        ],
        compiler_params=pltpu.CompilerParams(collective_id=0, has_side_effects=True),
        name="gather_attend",
    )(pair_in, pair_shift, pair_out, bin_states, w_query, w_keyval, contacts)

    p = lax.axis_index("pb")
    k = lax.axis_index("ka")
    start = ((p * block + k * offsets - HALF_BAND) // block).astype(jnp.int32).reshape(1)
    num, stat = pl.pallas_call(
        functools.partial(redo_kernel, tiles, pbn),
        out_shape=(
            jax.ShapeDtypeStruct((block, hc), BF16),
            jax.ShapeDtypeStruct((block // 128, 16, 128), BF16),
        ),
        in_specs=[smem, vmem, smem, smem, smem, hbm, hbm, hbm, hbm, hbm],
        out_specs=(hbm, hbm),
        scratch_shapes=[
            pltpu.VMEM((HEADS, SEGS, 8, 128), F32),
            pltpu.VMEM((128, offsets), jnp.int32),
            pltpu.VMEM((128, hc), BF16),
            pltpu.VMEM((window, 2 * hc), BF16),
            pltpu.VMEM((HEADS, 128, (tiles + 8) * 128), F32),
            pltpu.VMEM((HEADS, 128, 128), F32),
            pltpu.VMEM((HEADS, 128, (tiles + 4) * 128), F32),
            pltpu.VMEM((HEADS, 128, 256), F32),
            pltpu.VMEM((128, hc), BF16),
            pltpu.VMEM((16, 128), BF16),
            pltpu.SemaphoreType.DMA,
        ],
        input_output_aliases={8: 0, 9: 1},
        name="redo",
    )(start, odd, pair_in, pair_shift, pair_out, contacts, q_blk, win, num, stat)

    att = pl.pallas_call(
        functools.partial(reduce_kernel, pbn, kan),
        out_shape=jax.ShapeDtypeStruct((rows, hc), BF16),
        in_specs=[vmem, vmem],
        out_specs=vmem,
        scratch_shapes=[
            pltpu.VMEM((kan, rows, hc), BF16),
            pltpu.VMEM((kan, 16, 128), BF16),
            pltpu.SemaphoreType.DMA((kan,)),
            pltpu.SemaphoreType.DMA((kan,)),
            pltpu.SemaphoreType.DMA((kan,)),
            pltpu.SemaphoreType.DMA((kan,)),
        ],
        compiler_params=pltpu.CompilerParams(collective_id=1, has_side_effects=True),
        name="reduce_rows",
    )(num, stat)
    return jnp.dot(att, w_out, preferred_element_type=F32).astype(BF16)


def solution(mesh):
    placed = (P(("pb", "ka"), None), P("pb", "ka"), P(), P(), P(), P(), P(), P())
    return jax.shard_map(
        functools.partial(shards, mesh.shape["pb"], mesh.shape["ka"]),
        mesh=mesh, in_specs=placed, out_specs=P(("pb", "ka"), None), check_vma=False,
    )
```

```python
import functools
import jax
import jax.numpy as jnp
from jax import lax
from jax.experimental import pallas as pl
from jax.experimental.pallas import tpu as pltpu
from jax.sharding import PartitionSpec as P

HEADS = 2
HEAD_DIM = 128
PAIR_HIDDEN = 32
HALF_BAND = 8192
SEGS = 16
ROOT = HEAD_DIM**0.5
LOG2E = 1.4426950408889634
NEG = -1e30
MESH = pl.DeviceIdType.MESH
F32 = jnp.float32
BF16 = jnp.bfloat16


def pick(table, low):
    dims = lax.GatherDimensionNumbers(
        offset_dims=(), collapsed_slice_dims=(1,), start_index_map=(1,),
        operand_batching_dims=(0,), start_indices_batching_dims=(0,),
    )
    return lax.gather(
        table, low[:, :, None], dims, slice_sizes=(1, 1),
        mode=lax.GatherScatterMode.PROMISE_IN_BOUNDS,
    )


def shear(x):
    return pltpu.roll(x, 0, 1, stride=1, stride_axis=0)


def build_table(pin_ref, psh_ref, pout_ref, tab):
    ids = (
        lax.broadcasted_iota(jnp.int32, (SEGS, 128), 0) * 128
        + lax.broadcasted_iota(jnp.int32, (SEGS, 128), 1)
    )
    logc = jnp.log(1.0 + ids.astype(F32))
    for h in range(HEADS):
        summed = jnp.zeros((SEGS, 128), F32)
        for u in range(PAIR_HIDDEN):
            inner = pin_ref[h, u] * logc + psh_ref[h, u]
            summed = summed + pout_ref[h, u] * (inner / (1.0 + jnp.exp(-inner)))
        summed = summed * ROOT
        for s in range(SEGS):
            tab[h, s] = jnp.broadcast_to(summed[s : s + 1], (8, 128))


def message(rows, tops, sums, num_ref, stat_ref):
    lanes = lax.broadcasted_iota(jnp.int32, (128, 128), 1)
    stats = jnp.zeros((128, 128), F32)
    for h in range(HEADS):
        num_ref[rows, 128 * h : 128 * h + 128] = sums[h][:, 0:128].astype(BF16)
        for n, full in enumerate((tops[h] * (1.0 / ROOT), sums[h][:, 128:256])):
            for part in range(3):
                piece = full.astype(BF16).astype(F32)
                stats = jnp.where(lanes == h * 6 + n * 3 + part, piece, stats)
                full = full - piece
    stat_ref[...] = stats.T[0:16, :].astype(BF16)


def main_kernel(
    pbn, kan, pin_ref, psh_ref, pout_ref, x_hbm, wq_hbm, wkv_hbm, con_hbm,
    num_ref, stat_ref, odd_ref, q_out, win_out,
    x, wq, wkv, con, qs, kvs, qall, win, tab, bias, sbuf, wbuf, tops, alpha, acc,
    in_sem, con_sem, q_send, q_recv, kv_send, kv_recv, f_send, f_recv, out_sem,
):
    p = lax.axis_index("pb")
    k = lax.axis_index("ka")
    rows = x.shape[0]
    block = rows * kan
    tiles = con.shape[1] // 128
    partner = p + 1 - 2 * (p % 2)
    odd = p % 2
    first = p + 4 * k - 16
    pad = 4
    active = (first >= -4) & (first < pbn)

    loads = [
        pltpu.make_async_copy(x_hbm, x, in_sem.at[0]),
        pltpu.make_async_copy(wkv_hbm, wkv, in_sem.at[1]),
        pltpu.make_async_copy(wq_hbm, wq, in_sem.at[2]),
    ]
    for c in loads:
        c.start()

    def con_load(r):
        at = pl.ds(r * 128, 128)
        return pltpu.make_async_copy(con_hbm.at[at], con.at[at], con_sem.at[r])

    def dest(kd, m):
        pd = p - 4 * kd + 16 - 2 * m
        return pd, (pd >= 0) & (pd < pbn)

    def has(m):
        b = first + 2 * m
        return (b >= 0) & (b < pbn)

    barrier = pltpu.get_barrier_semaphore()
    for i in range(1, kan):
        pl.semaphore_signal(
            barrier, inc=1, device_id=(p, lax.rem(k + i, kan)), device_id_type=MESH
        )
    pl.semaphore_signal(barrier, inc=1, device_id=(partner, k), device_id_type=MESH)
    for m in range(3):
        b = first + 2 * m
        for i in range(kan):
            own = (b == p) & (i == 0)

            @pl.when(has(m) & jnp.logical_not(own))
            def _(b=b, i=i):
                pl.semaphore_signal(
                    barrier, inc=1, device_id=(b, lax.rem(k + i, kan)), device_id_type=MESH
                )

    expected = kan
    for i in range(kan):
        kd = lax.rem(k + i, kan)
        for m in range(3):
            pd, ok = dest(kd, m)
            own = (pd == p) & (i == 0)
            expected = expected + jnp.where(ok & jnp.logical_not(own), 1, 0)

    @pl.when(active)
    def _():
        build_table(pin_ref, psh_ref, pout_ref, tab)
        edge = jnp.full((block, (pad + 1) * 128), NEG, F32)
        for h in range(HEADS):
            bias[h, :, 0 : (pad + 1) * 128] = edge
            bias[h, :, (pad + tiles) * 128 : (2 * pad + tiles) * 128] = edge[:, 128:]
        tops[...] = jnp.full(tops.shape, NEG, F32)
        acc[...] = jnp.zeros(acc.shape, F32)

    loads[0].wait()
    loads[1].wait()
    for r in range(4):
        con_load(r).start()
    kvs[...] = jnp.dot(x[...], wkv[...], preferred_element_type=F32).astype(BF16)
    loads[2].wait()
    qs[...] = jnp.dot(x[...], wq[...], preferred_element_type=F32).astype(BF16)
    pl.semaphore_wait(barrier, expected)

    def q_copy(i):
        kd = lax.rem(k + i, kan)
        return pltpu.make_async_remote_copy(
            src_ref=qs, dst_ref=qall.at[pl.ds(k * rows, rows)],
            send_sem=q_send.at[i], recv_sem=q_recv,
            device_id=(p, kd), device_id_type=MESH,
        )

    def kv_rows(m):
        return win.at[pl.ds(2 * m * block + k * rows, rows)]

    def kv_copy(i, m, pd, kd):
        return pltpu.make_async_remote_copy(
            src_ref=kvs, dst_ref=kv_rows(m),
            send_sem=kv_send.at[i, m], recv_sem=kv_recv.at[m],
            device_id=(pd, kd), device_id_type=MESH,
        )

    def send_kv(m):
        for i in range(kan):
            kd = lax.rem(k + i, kan)
            pd, ok = dest(kd, m)
            own = (pd == p) & (i == 0)

            @pl.when(ok & jnp.logical_not(own))
            def _(i=i, m=m, pd=pd, kd=kd):
                kv_copy(i, m, pd, kd).start()

            if i == 0:

                @pl.when(ok & own)
                def _(m=m):
                    pltpu.make_async_copy(kvs, kv_rows(m), kv_recv.at[m]).start()

    def wanted(i):
        b0 = p + 4 * lax.rem(k + i, kan) - 16
        return (b0 >= -4) & (b0 < pbn)

    for i in range(1, kan):

        @pl.when(wanted(i))
        def _(i=i):
            q_copy(i).start()

    @pl.when(active)
    def _():
        pltpu.make_async_copy(qs, qall.at[pl.ds(k * rows, rows)], q_recv).start()

    send_kv(0)
    send_kv(1)
    send_kv(2)

    def fwd(slot):
        m = slot + 1 - odd
        return pltpu.make_async_remote_copy(
            src_ref=win.at[pl.ds(2 * m * block, block)],
            dst_ref=win.at[pl.ds((2 * slot + 1) * block, block)],
            send_sem=f_send.at[slot], recv_sem=f_recv.at[slot],
            device_id=(partner, k), device_id_type=MESH,
        )

    def in_block(m):
        part = win.at[pl.ds(2 * m * block, block)]
        return pltpu.make_async_remote_copy(
            src_ref=part, dst_ref=part, send_sem=kv_send.at[0, m], recv_sem=kv_recv.at[m],
            device_id=(partner, k), device_id_type=MESH,
        )

    def keep(j):
        at = pl.ds(j * block, block)
        return pltpu.make_async_copy(win.at[at], win_out.at[at], out_sem.at[j])

    lanes = lax.broadcasted_iota(jnp.int32, (128, 128), 1)
    subl = lax.broadcasted_iota(jnp.int32, (128, 128), 0)
    here = lanes >= subl

    @pl.when(active)
    def _():
        tables = [tab[h, 0] for h in range(HEADS)]
        near = jnp.where(k == 4, 0, jnp.where(k == 3, tiles - 1, -1))
        second = jnp.where(k == 4, 1, jnp.where(k == 3, tiles - 2, -1))

        for r in range(4):
            con_load(r).wait()

        def put(h, row, at, g, val):
            where = pl.ds(row, 8)
            mask = here[8 * g : 8 * g + 8]
            at = at + pad * 128
            pltpu.store(bias.at[h, where, pl.ds(at, 128)], val, mask=mask)
            pltpu.store(bias.at[h, where, pl.ds(at + 128, 128)], val, mask=jnp.logical_not(mask))

        def look_rows(r, every):
            at_r = pl.multiple_of(r * 128, 128)
            band = pl.ds(at_r, 128)
            def look(it, every):
                for u in range(4):
                    j = it * 4 + u
                    at = pl.multiple_of(j * 128, 128)
                    c = con[band, pl.ds(at, 128)]
                    some = functools.reduce(
                        jnp.bitwise_or, [c[8 * g : 8 * g + 8] for g in range(16)]
                    )
                    beyond = jnp.where(j == near, 0, jnp.where(j == second, -512, -128))
                    every = every | (some & beyond)
                    low = shear(c & 127)
                    for g in range(16):
                        for h in range(HEADS):
                            put(h, at_r + 8 * g, at, g, pick(tables[h], low[8 * g : 8 * g + 8]))
                return every

            every = lax.fori_loop(0, tiles // 4, look, every)

            def further(j, count):
                at = pl.multiple_of(j * 128, 128)
                c = shear(con[band, pl.ds(at, 128)])
                for g in range(16):
                    low = c[8 * g : 8 * g + 8] & 127
                    row = c[8 * g : 8 * g + 8] >> 7
                    got = [pick(tables[h], low) for h in range(HEADS)]
                    for u in range(1, count):
                        hit = row == u
                        for h in range(HEADS):
                            got[h] = jnp.where(hit, pick(tab[h, u], low), got[h])
                    for h in range(HEADS):
                        put(h, at_r + 8 * g, at, g, got[h])

            @pl.when(near >= 0)
            def _():
                further(near, SEGS)
                further(second, 4)

            return every

        odd_ref[...] = lax.fori_loop(0, 4, look_rows, jnp.zeros((8, 128), jnp.int32))

    whole = pltpu.make_async_remote_copy(
        src_ref=qall, dst_ref=qall, send_sem=q_send.at[0], recv_sem=q_recv,
        device_id=(partner, k), device_id_type=MESH,
    )
    q_keep = pltpu.make_async_copy(qall, q_out, out_sem.at[5])

    @pl.when(active)
    def _():
        whole.wait_recv()
        q_keep.start()

    ones = jnp.ones((block, 128), BF16)

    def attend(j, outside):
        at_k = pl.multiple_of(j * block, block)
        for h in range(HEADS):
            keys = win[pl.ds(at_k, block), 128 * h : 128 * h + 128]
            s = jnp.dot(
                qall[:, 128 * h : 128 * h + 128], keys.T, preferred_element_type=F32
            )
            for r in range(4):
                band = slice(128 * r, 128 * r + 128)
                used = [i for i in range(4) if not outside(i, r)]
                most = None
                for i in used:
                    at = pl.multiple_of((pad + 4 * j + i - r) * 128, 128)
                    part = s[band, 128 * i : 128 * i + 128] + bias[h, band, pl.ds(at, 128)]
                    sbuf[h, band, 128 * i : 128 * i + 128] = part
                    most = part if most is None else jnp.maximum(most, part)
                top = tops[h, band, :]
                new = jnp.maximum(top, jnp.max(most, axis=1, keepdims=True))
                alpha[h, band, :] = jnp.exp2((top - new) * (LOG2E / ROOT))
                tops[h, band, :] = new
                for i in range(4):
                    spot = (h, band, slice(128 * i, 128 * i + 128))
                    if i in used:
                        wbuf[spot] = jnp.exp2((sbuf[spot] - new) * (LOG2E / ROOT)).astype(BF16)
                    else:
                        wbuf[spot] = jnp.zeros((128, 128), BF16)
            vals = win[pl.ds(at_k, block), 256 + 128 * h : 384 + 128 * h]
            new = jnp.dot(
                wbuf[h], jnp.concatenate([vals, ones], 1), preferred_element_type=F32
            )
            a = alpha[h]
            acc[h] = acc[h] * jnp.concatenate([a, a], 1) + new

    def step(it, _):
        j = lax.rem(2 * it, 5)
        b = first + j

        @pl.when((b >= 0) & (b < pbn))
        def _():
            @pl.when(it < 3)
            def _():
                in_block(it).wait_recv()
                slot = it - 1 + odd

                @pl.when((slot >= 0) & (slot < 2))
                def _():
                    fwd(slot).start()

            @pl.when(it >= 3)
            def _():
                fwd(it - 3).wait_recv()

            keep(j).start()

            @pl.when(j == 0)
            def _():
                attend(j, lambda i, r: i < r)

            @pl.when(j == 4)
            def _():
                attend(j, lambda i, r: i > r)

            @pl.when((j > 0) & (j < 4))
            def _():
                attend(j, lambda i, r: False)

        return 0

    lax.fori_loop(0, 5, step, 0)

    @pl.when(active)
    def _():
        def finish(r, _):
            band = pl.ds(pl.multiple_of(r * 128, 128), 128)
            message(
                band, [tops[h, band, :] for h in range(HEADS)],
                [acc[h, band, :] for h in range(HEADS)], num_ref, stat_ref.at[r],
            )
            return 0

        lax.fori_loop(0, 4, finish, 0)

    @pl.when(jnp.logical_not(active))
    def _():
        odd_ref[...] = jnp.zeros((8, 128), jnp.int32)
        num_ref[...] = jnp.zeros(num_ref.shape, BF16)
        stat_ref[...] = jnp.zeros(stat_ref.shape, BF16)
        for r in range(4):
            con_load(r).wait()

    def drain(j, _):
        b = first + j

        @pl.when((b >= 0) & (b < pbn))
        def _():
            keep(j).wait()

        return 0

    lax.fori_loop(0, 5, drain, 0)

    @pl.when(active)
    def _():
        q_keep.wait()

    for slot in range(2):
        b_out = first + 2 * (slot + 1 - odd)

        @pl.when((b_out >= 0) & (b_out < pbn))
        def _(slot=slot):
            fwd(slot).wait_send()

    for i in range(kan):
        kd = lax.rem(k + i, kan)
        for m in range(3):
            pd, ok = dest(kd, m)
            own = (pd == p) & (i == 0)

            @pl.when(ok & jnp.logical_not(own))
            def _(i=i, m=m, pd=pd, kd=kd):
                kv_copy(i, m, pd, kd).wait_send()

        if i:

            @pl.when(wanted(i))
            def _(i=i):
                q_copy(i).wait_send()


def redo_kernel(
    tiles, blocks, start_ref, odd_ref, pin_ref, psh_ref, pout_ref, con_hbm, q_hbm, win_hbm, num_in,
    stat_in, num_out, stat_out, tab, con, q, win, bias, smax, sbuf, acc, num, stat, sem,
):
    first = start_ref[0]
    pad = 4

    @pl.when(jnp.max(odd_ref[...].astype(F32)) > 0.5)
    def _():
        lanes = lax.broadcasted_iota(jnp.int32, (128, 128), 1)
        subl = lax.broadcasted_iota(jnp.int32, (128, 128), 0)
        here = lanes >= subl
        build_table(pin_ref, psh_ref, pout_ref, tab)
        lo = jnp.maximum(0, -first)
        hi = jnp.minimum(tiles // 4 + 1, blocks - first)
        edge = jnp.full((128, pad * 128), NEG, F32)
        for h in range(HEADS):
            bias[h, :, 0 : pad * 128] = edge
            bias[h, :, (pad + tiles) * 128 : (2 * pad + tiles) * 128] = edge

        def fetch(src, dst):
            c = pltpu.make_async_copy(src, dst, sem)
            c.start()
            c.wait()

        def load_win(j, _):
            at = pl.ds(pl.multiple_of(j * 512, 512), 512)
            fetch(win_hbm.at[at], win.at[at])
            return 0

        lax.fori_loop(lo, hi, load_win, 0)
        ones = jnp.ones((512, 128), BF16)

        def rows(rb, _):
            band = pl.ds(pl.multiple_of(rb * 128, 128), 128)
            fetch(con_hbm.at[band], con)
            fetch(q_hbm.at[band], q)
            smax[...] = jnp.full(smax.shape, NEG, F32)
            acc[...] = jnp.zeros(acc.shape, F32)

            def look(j, _):
                at = pl.multiple_of(j * 128, 128)
                c = shear(con[:, pl.ds(at, 128)])

                def row(s, _):
                    for g in range(16):
                        part = c[8 * g : 8 * g + 8]
                        for h in range(HEADS):
                            spot = (h, slice(8 * g, 8 * g + 8), pl.ds(at + pad * 128, 128))
                            bias[spot] = jnp.where(
                                (part >> 7) == s, pick(tab[h, s], part & 127), bias[spot]
                            )
                    return 0

                lax.fori_loop(0, SEGS, row, 0)
                return 0

            lax.fori_loop(0, tiles, look, 0)

            def score(j, _):
                for h in range(HEADS):
                    keys = win[
                        pl.ds(pl.multiple_of(j * 512, 512), 512), 128 * h : 128 * h + 128
                    ]
                    s = jnp.dot(
                        q[:, 128 * h : 128 * h + 128], keys.T, preferred_element_type=F32
                    )
                    top = smax[h]
                    for i in range(4):
                        at = pl.multiple_of((pad + 4 * j + i - rb) * 128, 128)
                        b = jnp.where(
                            here, bias[h, :, pl.ds(at, 128)], bias[h, :, pl.ds(at - 128, 128)]
                        )
                        part = s[:, 128 * i : 128 * i + 128] + b
                        sbuf[h, :, pl.ds(pl.multiple_of((4 * j + i) * 128, 128), 128)] = part
                        top = jnp.maximum(top, part)
                    smax[h] = top
                return 0

            lax.fori_loop(lo, hi, score, 0)
            for h in range(HEADS):
                smax[h] = jnp.broadcast_to(jnp.max(smax[h], axis=1, keepdims=True), (128, 128))

            def weigh(j, _):
                for h in range(HEADS):
                    vals = win[
                        pl.ds(pl.multiple_of(j * 512, 512), 512), 256 + 128 * h : 384 + 128 * h
                    ]
                    w = []
                    for i in range(4):
                        s = sbuf[h, :, pl.ds(pl.multiple_of((4 * j + i) * 128, 128), 128)]
                        w.append(jnp.exp2((s - smax[h]) * (LOG2E / ROOT)).astype(BF16))
                    acc[h] += jnp.dot(
                        jnp.concatenate(w, 1), jnp.concatenate([vals, ones], 1),
                        preferred_element_type=F32,
                    )
                return 0

            lax.fori_loop(lo, hi, weigh, 0)
            message(
                slice(0, 128), [smax[h] for h in range(HEADS)],
                [acc[h] for h in range(HEADS)], num, stat,
            )
            fetch(num, num_out.at[band])
            fetch(stat, stat_out.at[rb])
            return 0

        lax.fori_loop(0, 4, rows, 0)


def reduce_kernel(pbn, kan, num_ref, stat_ref, out_ref, nums, stats, send, recv, st_send, st_recv):
    p = lax.axis_index("pb")
    k = lax.axis_index("ka")
    rows = out_ref.shape[0]

    def active(kd):
        b0 = p + 4 * kd - 16
        return (b0 >= -4) & (b0 < pbn)

    barrier = pltpu.get_barrier_semaphore()
    for i in range(1, kan):
        kd = lax.rem(k + i, kan)

        @pl.when(active(kd))
        def _(kd=kd):
            pl.semaphore_signal(barrier, inc=1, device_id=(p, kd), device_id_type=MESH)

    def copies(i):
        kd = lax.rem(k + i, kan)
        to = {"device_id": (p, kd), "device_id_type": MESH}
        return (
            pltpu.make_async_remote_copy(
                src_ref=stat_ref.at[kd // 2], dst_ref=stats.at[i],
                send_sem=st_send.at[i], recv_sem=st_recv.at[i], **to,
            ),
            pltpu.make_async_remote_copy(
                src_ref=num_ref.at[pl.ds(kd * rows, rows)], dst_ref=nums.at[i],
                send_sem=send.at[i], recv_sem=recv.at[i], **to,
            ),
        )

    @pl.when(active(k))
    def _():
        pl.semaphore_wait(barrier, kan - 1)
        for i in range(1, kan):
            for c in copies(i):
                c.start()

    nums[0] = num_ref[pl.ds(pl.multiple_of(k * rows, rows), rows), :]
    stats[0] = stat_ref[k // 2]
    for i in range(1, kan):
        src = lax.rem(k + kan - i, kan)

        @pl.when(active(src))
        def _(i=i):
            copies(i)[0].wait_recv()

        @pl.when(jnp.logical_not(active(src)))
        def _(i=i):
            nums[i] = jnp.zeros(nums.shape[1:], BF16)
            stats[i] = jnp.zeros(stats.shape[1:], BF16)

    shares = []
    for h in range(HEADS):
        tops, tots = [], []
        for i in range(kan):
            st = stats[i].astype(F32)
            live = active(lax.rem(k + kan - i, kan))
            a = 6 * h
            top = st[a : a + 1] + st[a + 1 : a + 2] + st[a + 2 : a + 3]
            tops.append(jnp.where(live, top, NEG))
            tots.append(st[a + 3 : a + 4] + st[a + 4 : a + 5] + st[a + 5 : a + 6])
        top = functools.reduce(jnp.maximum, tops)
        w = [jnp.exp(t - top) for t in tops]
        tot = functools.reduce(jnp.add, [a * b for a, b in zip(w, tots)])
        shares += [a / tot for a in w]
    cols = jnp.concatenate(shares + [jnp.zeros((128 - len(shares), 128), F32)], 0).T
    cols = jnp.where(lax.rem(k, 2) == 0, cols[0:rows], cols[rows : 2 * rows])

    for i in range(1, kan):

        @pl.when(active(lax.rem(k + kan - i, kan)))
        def _(i=i):
            copies(i)[1].wait_recv()

    for h in range(HEADS):
        num = jnp.zeros((rows, HEAD_DIM), F32)
        for i in range(kan):
            at = kan * h + i
            num = num + cols[:, at : at + 1] * nums[i, :, 128 * h : 128 * h + 128].astype(F32)
        out_ref[:, 128 * h : 128 * h + 128] = num.astype(BF16)

    @pl.when(active(k))
    def _():
        for i in range(1, kan):
            for c in copies(i):
                c.wait_send()


def shards(pbn, kan, bin_states, contacts, w_query, w_keyval, pair_in, pair_shift, pair_out, w_out):
    vmem = pl.BlockSpec(memory_space=pltpu.VMEM)
    smem = pl.BlockSpec(memory_space=pltpu.SMEM)
    hbm = pl.BlockSpec(memory_space=pl.ANY)
    rows, width = bin_states.shape
    block, offsets = contacts.shape
    hc = HEADS * HEAD_DIM
    window = block + offsets
    tiles = offsets // 128
    num, stat, odd, q_blk, win = pl.pallas_call(
        functools.partial(main_kernel, pbn, kan),
        out_shape=(
            jax.ShapeDtypeStruct((block, hc), BF16),
            jax.ShapeDtypeStruct((block // 128, 16, 128), BF16),
            jax.ShapeDtypeStruct((8, 128), jnp.int32),
            jax.ShapeDtypeStruct((block, hc), BF16),
            jax.ShapeDtypeStruct((window, 2 * hc), BF16),
        ),
        in_specs=[smem, smem, smem, hbm, hbm, hbm, hbm],
        out_specs=(vmem, vmem, vmem, hbm, hbm),
        scratch_shapes=[
            pltpu.VMEM((rows, width), BF16),
            pltpu.VMEM((width, hc), BF16),
            pltpu.VMEM((width, 2 * hc), BF16),
            pltpu.VMEM((block, offsets), jnp.int32),
            pltpu.VMEM((rows, hc), BF16),
            pltpu.VMEM((rows, 2 * hc), BF16),
            pltpu.VMEM((block, hc), BF16),
            pltpu.VMEM((window, 2 * hc), BF16),
            pltpu.VMEM((HEADS, SEGS, 8, 128), F32),
            pltpu.VMEM((HEADS, block, (tiles + 8) * 128), F32),
            pltpu.VMEM((HEADS, block, block), F32),
            pltpu.VMEM((HEADS, block, block), BF16),
            pltpu.VMEM((HEADS, block, 128), F32),
            pltpu.VMEM((HEADS, block, 128), F32),
            pltpu.VMEM((HEADS, block, 256), F32),
            pltpu.SemaphoreType.DMA((3,)),
            pltpu.SemaphoreType.DMA((4,)),
            pltpu.SemaphoreType.DMA((kan,)),
            pltpu.SemaphoreType.DMA,
            pltpu.SemaphoreType.DMA((kan, 3)),
            pltpu.SemaphoreType.DMA((3,)),
            pltpu.SemaphoreType.DMA((2,)),
            pltpu.SemaphoreType.DMA((2,)),
            pltpu.SemaphoreType.DMA((6,)),
        ],
        compiler_params=pltpu.CompilerParams(collective_id=0, has_side_effects=True),
        name="gather_attend",
    )(pair_in, pair_shift, pair_out, bin_states, w_query, w_keyval, contacts)

    p = lax.axis_index("pb")
    k = lax.axis_index("ka")
    start = ((p * block + k * offsets - HALF_BAND) // block).astype(jnp.int32).reshape(1)
    num, stat = pl.pallas_call(
        functools.partial(redo_kernel, tiles, pbn),
        out_shape=(
            jax.ShapeDtypeStruct((block, hc), BF16),
            jax.ShapeDtypeStruct((block // 128, 16, 128), BF16),
        ),
        in_specs=[smem, vmem, smem, smem, smem, hbm, hbm, hbm, hbm, hbm],
        out_specs=(hbm, hbm),
        scratch_shapes=[
            pltpu.VMEM((HEADS, SEGS, 8, 128), F32),
            pltpu.VMEM((128, offsets), jnp.int32),
            pltpu.VMEM((128, hc), BF16),
            pltpu.VMEM((window, 2 * hc), BF16),
            pltpu.VMEM((HEADS, 128, (tiles + 8) * 128), F32),
            pltpu.VMEM((HEADS, 128, 128), F32),
            pltpu.VMEM((HEADS, 128, (tiles + 4) * 128), F32),
            pltpu.VMEM((HEADS, 128, 256), F32),
            pltpu.VMEM((128, hc), BF16),
            pltpu.VMEM((16, 128), BF16),
            pltpu.SemaphoreType.DMA,
        ],
        input_output_aliases={8: 0, 9: 1},
        name="redo",
    )(start, odd, pair_in, pair_shift, pair_out, contacts, q_blk, win, num, stat)

    att = pl.pallas_call(
        functools.partial(reduce_kernel, pbn, kan),
        out_shape=jax.ShapeDtypeStruct((rows, hc), BF16),
        in_specs=[vmem, vmem],
        out_specs=vmem,
        scratch_shapes=[
            pltpu.VMEM((kan, rows, hc), BF16),
            pltpu.VMEM((kan, 16, 128), BF16),
            pltpu.SemaphoreType.DMA((kan,)),
            pltpu.SemaphoreType.DMA((kan,)),
            pltpu.SemaphoreType.DMA((kan,)),
            pltpu.SemaphoreType.DMA((kan,)),
        ],
        compiler_params=pltpu.CompilerParams(collective_id=1, has_side_effects=True),
        name="reduce_rows",
    )(num, stat)
    return jnp.dot(att, w_out, preferred_element_type=F32).astype(BF16)


def solution(mesh):
    placed = (P(("pb", "ka"), None), P("pb", "ka"), P(), P(), P(), P(), P(), P())
    return jax.shard_map(
        functools.partial(shards, mesh.shape["pb"], mesh.shape["ka"]),
        mesh=mesh, in_specs=placed, out_specs=P(("pb", "ka"), None), check_vma=False,
    )
```
